512 devices in a mesh: lat: 128 (over z, y, core), tok: 4 (over x).
Axes of the slice: x: 4, y: 8, z: 8, core: 2. Of those that a mesh axis runs over, the one named last changes fastest.
Arguments:
- resid_stream: bfloat16 [384, 8192], P('lat', 'tok'), may hold values from -6 to 6
- enc_weight: bfloat16 [16384, 8192], P('lat', 'tok'), may hold values from -0.0625 to 0.0625
- enc_bias: float32 [16384], P('lat'), may hold values from -3 to 3
- dec_weight: bfloat16 [16384, 8192], P('lat', 'tok'), may hold values from -0.75 to 0.75
- dec_bias: float32 [8192], P('tok'), may hold values from -3 to 3
- active_ids: int32 [384, 64], replicated, may hold values from 0 to 16383, as said below
- active_count: int32 [384], replicated, may hold values from 32 to 64, as said below
Outputs:
- pre_acts: float32 [384, 16384], P(None, 'lat')
- residual: bfloat16 [384, 8192], P('lat', 'tok')
- grad_enc: bfloat16 [16384, 8192], P('lat', 'tok')
- grad_dec: bfloat16 [16384, 8192], P('lat', 'tok')
The draws below stay inside these ranges and needn't reach their ends.
Inputs may be any that keep to these rules, and one draw needn't show every extreme that they name: `active_ids`: within a row all 64 entries are different latents; entries past the row's count are ordinary latent numbers that are to be ignored; some latent shards are named far more often than others. `active_count`: some row has 64 valid entries and some has 32.
All inputs are finite; a program needn't handle non-finite values.
Results may differ from the reference program's by a relative error of at most 0.0059.
Values may be sent and summed in bfloat16 or wider, within the bound.
A program may use at most 64 MiB of HBM per device.

```python
import jax
import jax.numpy as jnp
from jax import lax

D = 8192
K = 64
LAT_DEV = 128
LATENTS = 16384
TOKENS = 384


def active_lists(key):
    key = jax.random.fold_in(key, 7321)
    key_hot, key_base, key_count = jax.random.split(key, 3)
    hotness = jax.random.randint(key_hot, (LATENTS // LAT_DEV,), 0, 4)
    base_score = jax.random.randint(key_base, (TOKENS, LATENTS), 0, 16384)
    score = (base_score + jnp.repeat(hotness, LAT_DEV)[None, :] * 4096) * LATENTS
    score = score + jnp.arange(LATENTS, dtype=jnp.int32)[None, :]
    score = score.at[0, 0].set(1073741824).at[0, LATENTS - 1].set(1073741823)
    picked = lax.top_k(score, K)[1].astype(jnp.int32)
    counts = jax.random.randint(key_count, (TOKENS,), K // 2, K + 1)
    counts = counts.at[0].set(K).at[TOKENS - 1].set(K // 2)
    return (picked, counts.astype(jnp.int32))


def draw_active_ids(key, part):
    return active_lists(key)[0]


def draw_active_count(key, part):
    return active_lists(key)[1]


def shard_levels(key, extent, pieces, low, top_value):
    gain = 1.0
    for dim, shards_of in pieces:
        heights = jax.random.uniform(jax.random.fold_in(jax.random.fold_in(key, 6), dim), (shards_of,), jnp.float32, low / len(pieces), top_value / len(pieces))
        gain = gain * jnp.repeat(jnp.exp(heights), extent[dim] // shards_of).reshape((-1,) + (1,) * (len(extent) - 1 - dim))
    return gain


def bell_draw(rng, extent, scale, reach, pieces=(), kind=jnp.bfloat16):
    values = jax.random.normal(rng, extent, jnp.float32) * scale
    if len(pieces) > 0:
        values = shard_levels(rng, extent, pieces, -0.22, 0.18) * values
    return jnp.clip(values, min=-reach, max=reach).astype(kind)


def setup_inputs(seed: int = 0) -> dict:
    key_of = jax.random.split(jax.random.key(seed), 8)
    return {
        "resid_stream": bell_draw(key_of[0], (TOKENS, D), 1.0, 6.0, ((0, 128), (1, 4))),
        "enc_weight": bell_draw(key_of[1], (LATENTS, D), D ** -0.5, 0.0625, ((0, 128), (1, 4))),
        "enc_bias": bell_draw(key_of[2], (LATENTS,), 0.5, 3.0, ((0, 128),), jnp.float32),
        "dec_weight": bell_draw(key_of[3], (LATENTS, D), K ** -0.5, 0.75, ((0, 128), (1, 4))),
        "dec_bias": bell_draw(key_of[4], (D,), 0.5, 3.0, ((0, 4),), jnp.float32),
        "active_ids": draw_active_ids(jax.random.fold_in(key_of[7], 71), 0),
        "active_count": draw_active_count(jax.random.fold_in(key_of[7], 71), 0),
    }


def reference(resid_stream, enc_weight, enc_bias, dec_weight, dec_bias, active_ids, active_count):
    pre_acts = jnp.dot(resid_stream, enc_weight.T, preferred_element_type=jnp.float32) + enc_bias[None, :]
    in_list = (jnp.arange(K, dtype=jnp.int32)[None, :] < active_count[:, None]).astype(jnp.float32)
    row_ids = jnp.broadcast_to(jnp.arange(TOKENS, dtype=jnp.int32)[:, None], (TOKENS, K))
    act_mask = jnp.zeros((TOKENS, LATENTS), jnp.float32).at[row_ids, active_ids].add(in_list)
    activations = (pre_acts * act_mask).astype(jnp.bfloat16)
    rebuilt = jnp.dot(activations, dec_weight, preferred_element_type=jnp.float32) + dec_bias[None, :]
    residual = (rebuilt - resid_stream.astype(jnp.float32)).astype(jnp.bfloat16)
    grad_dec = (0.5 * jnp.dot(activations.T, residual, preferred_element_type=jnp.float32)).astype(jnp.bfloat16)
    back_terms = jnp.dot(residual, dec_weight.T, preferred_element_type=jnp.float32)
    act_grads = (0.5 * back_terms * act_mask).astype(jnp.bfloat16)
    grad_enc = jnp.dot(act_grads.T, resid_stream, preferred_element_type=jnp.float32).astype(jnp.bfloat16)
    return pre_acts, residual, grad_enc, grad_dec
```

```python
import functools
import math

import jax
import jax.numpy as jnp
from jax import lax
from jax.experimental import pallas as pl
from jax.experimental.pallas import tpu as pltpu
from jax.sharding import PartitionSpec as P

F32 = jnp.float32
BF16 = jnp.bfloat16
MESH = pl.DeviceIdType.MESH


def divisor(limit, by):
    s = 16
    m = (1 << s) // by + 1
    assert all((i * m) >> s == i // by for i in range(limit))
    return m, s


class Dims:
    def __init__(self, mesh, rows_own, width, lat_dev, top_count):
        self.X = mesh.shape["tok"]
        self.n = math.isqrt(mesh.shape["lat"] // 2)
        assert self.n * self.n * 2 == mesh.shape["lat"]
        self.own = rows_own
        self.rows = rows_own * mesh.shape["lat"]
        self.block = self.rows // self.n
        self.width = width // 2
        self.lanes = self.width // 128
        self.flat = rows_own * self.lanes
        self.lat = lat_dev
        self.top = top_count
        self.chunk = self.rows // self.X


def kernel(
    dm,
    x_ref, ids_ref, cnt_ref, eb_ref, db_ref, enc_ref, dec_ref,
    pre_out, res_out, ge_out, gd_out,
    F, R1, Xraw, XF, WE, WD, PS, PR, SUM, RX, mask, act_s, act_f, pre_s, pre_f,
    T, RB, Q, RQ, RES, RESF, ag_s, ag_f,
    send, recv, local,
):
    n, X, own, block, width, lanes, flat = dm.n, dm.X, dm.own, dm.block, dm.width, dm.lanes, dm.flat
    rows, lat, chunk, half = dm.rows, dm.lat, dm.chunk, dm.width // 2
    depth = n // 2
    L = lax.axis_index("lat")
    t = lax.axis_index("tok")
    c = lax.rem(L, 2)
    chip = L // 2
    y = lax.rem(chip, n)
    z = chip // n
    a = y + c * (z - y)
    b = z + c * (y - z)
    partner = L + 1 - 2 * c

    def lat_of(ap, bp):
        yy = ap + c * (bp - ap)
        zz = bp + c * (ap - bp)
        return (zz * n + yy) * 2 + c

    count = {"copy": 0, "local": 0}
    sends = []

    def wrap(v, m):
        return lax.rem(v + 2 * m, m)

    def remote(src, dst, lat_id, tok_id, recv_index=None):
        k = count["copy"]
        count["copy"] += 1
        r = k if recv_index is None else recv_index
        d = pltpu.make_async_remote_copy(
            src_ref=src, dst_ref=dst, send_sem=send.at[k], recv_sem=recv.at[r],
            device_id=(lat_id, tok_id), device_id_type=MESH,
        )
        return d

    def go(d):
        d.start()
        sends.append(d)
        return d

    def copy_local(src, dst):
        k = count["local"]
        count["local"] += 1
        d = pltpu.make_async_copy(src, dst, local.at[k])
        d.start()
        return d

    barrier = pltpu.get_barrier_semaphore()
    heard = 0

    def greet(lat_id, tok_id):
        pl.semaphore_signal(barrier, inc=1, device_id=(lat_id, tok_id), device_id_type=MESH)

    greet(partner, t)
    heard += 1
    for d in range(1, n):
        for other in (0, 1):
            dev = lat_of(wrap(a + d, n), b)
            greet(dev + other * (1 - 2 * c), t)
    heard += 2 * (n - 1)
    for s in (1, -1):
        greet(lat_of(a, wrap(b + s, n)), t)
    heard += 2
    for d in range(1, X):
        for dev in (L, partner):
            greet(dev, wrap(t + d, X))
    heard += 2 * (X - 1)

    xv = x_ref[...].astype(F32)
    for r in range(own):
        for j in range(2 * lanes):
            F[j // lanes, r * lanes + j % lanes : r * lanes + j % lanes + 1, :] = xv[
                r : r + 1, j * 128 : (j + 1) * 128
            ]

    pl.semaphore_wait(barrier, heard)

    recv1 = count["copy"]
    count["copy"] += 2 * n

    def slot1(pos, core):
        return pl.ds(pl.multiple_of((pos * 2 + core) * flat, 8), flat)

    go(remote(F.at[1 - c], R1.at[slot1(y + (1 - c) * (z - y), c)], partner, t, recv1 + c))
    for d in range(1, n):
        for h in (0, 1):
            pos = (y, z)[h]
            yy = wrap(y + d, n) if h == 0 else y
            zz = wrap(z + d, n) if h == 1 else z
            go(remote(F.at[h], R1.at[slot1(pos, c)], (zz * n + yy) * 2 + h, t, recv1 + 2 * d + c))
    mine = F[c]
    R1[slot1(a, c), :] = mine

    own_cols = pl.ds(pl.multiple_of(c * width, 128), width)
    far_cols = pl.ds(pl.multiple_of((1 - c) * width, 128), width)
    own_lats = pl.ds(pl.multiple_of(c * lat, lat), lat)
    w_local = [copy_local(enc_ref.at[:, own_cols], WE.at[own_lats]), copy_local(dec_ref.at[:, own_cols], WD.at[own_lats])]
    w_remote = [
        go(remote(enc_ref.at[:, far_cols], WE.at[own_lats], partner, t)),
        go(remote(dec_ref.at[:, far_cols], WD.at[own_lats], partner, t)),
    ]

    my_rows = pl.ds(pl.multiple_of(t * chunk, 8), chunk)
    cnt_row = cnt_ref[...].astype(F32)
    row_i = lax.broadcasted_iota(jnp.int32, (chunk, rows), 0) + t * chunk
    col_i = lax.broadcasted_iota(jnp.int32, (chunk, rows), 1)
    cnt_col = jnp.sum(
        jnp.where(row_i == col_i, jnp.broadcast_to(cnt_row, (chunk, rows)), 0.0), axis=1, keepdims=True
    )
    k_i = lax.broadcasted_iota(jnp.int32, (chunk, dm.top), 1).astype(F32)
    local_ids = jnp.where(k_i < cnt_col, ids_ref[my_rows, :] - L * lat, -1)
    lane_i = lax.broadcasted_iota(jnp.int32, (chunk, lat), 1)
    m = jnp.zeros((chunk, lat), F32)
    for k in range(dm.top):
        m = jnp.where(local_ids[:, k : k + 1] == lane_i, 1.0, m)
    mask[...] = m

    m1, s1 = divisor(rows, block)
    m2, s2 = divisor(block, block // n)
    i0 = lax.broadcasted_iota(jnp.int32, (rows, rows), 0)
    i1 = lax.broadcasted_iota(jnp.int32, (rows, rows), 1)
    hi = (i0 * m1) >> s1
    rest = i0 - hi * block
    mid = (rest * m2) >> s2
    low = rest - mid * (block // n)
    order = i0 + c * (mid * block + hi * (block // n) + low - i0)
    perm = jnp.where(order == i1, 1.0, 0.0).astype(BF16)

    def remote_wait(index):
        pltpu.make_async_remote_copy(
            src_ref=F.at[0], dst_ref=R1.at[pl.ds(0, flat)], send_sem=send.at[0], recv_sem=recv.at[index],
            device_id=(partner, t), device_id_type=MESH,
        ).wait_recv()

    remote_wait(recv1 + 1 - c)
    for d in range(1, n):
        for core in (0, 1):
            remote_wait(recv1 + 2 * d + core)
    my_block = pl.ds(pl.multiple_of(b * block, 16), block)
    for j in range(lanes):
        Xraw[my_block, j * 128 : (j + 1) * 128] = R1[pl.ds(j, block, stride=lanes), :].astype(BF16)

    def ring_gather(buf):
        def piece(blk, h):
            return buf.at[pl.ds(pl.multiple_of(blk * block, 16), block), pl.ds(h * half, half)]

        flying = {}

        def send_step(way, s, h):
            blk = wrap(b - way * (s - 1), n)
            flying[way, s, h] = go(remote(piece(blk, h), piece(blk, h), lat_of(a, wrap(b + way, n)), t))

        for s in range(1, depth + 1):
            for o in (0, 1):
                for way in (1, -1):
                    first = 0 if way == 1 else 1
                    h = first if o == 0 else 1 - first
                    if s > 1:
                        flying[way, s - 1, h].wait_recv()
                    if s < depth or h == first:
                        send_step(way, s, h)
        flying[1, depth, 0].wait_recv()
        flying[-1, depth, 1].wait_recv()

    ring_gather(Xraw)

    for w in w_local:
        w.wait()
    for w in w_remote:
        w.wait_recv()

    xp = jnp.dot(perm, Xraw[...], preferred_element_type=F32).astype(BF16)
    XF[c] = xp
    x_swap = go(remote(XF.at[c], XF.at[c], partner, t))

    def feature_sum(u, part):
        PS[u, 0] = part[:, :lat]
        PS[u, 1] = part[:, lat:]
        d = go(remote(PS.at[u, 1 - c], PR.at[u], partner, t))
        d.wait_recv()
        SUM[u] = PS[u, c] + PR[u]
        arrive = []
        for d in range(1, X):
            to = wrap(t + d, X)
            arrive.append(go(remote(SUM.at[u, pl.ds(pl.multiple_of(to * chunk, 8), chunk)], RX.at[u, d - 1], L, to)))
        total = SUM[u, my_rows, :]
        for d in range(1, X):
            arrive[d - 1].wait_recv()
            total = total + RX[u, d - 1]
        return total

    nt = (((1,), (1,)), ((), ()))
    tn = (((0,), (0,)), ((), ()))
    part = lax.dot_general(XF[c], WE[...], nt, preferred_element_type=F32)
    pre = feature_sum(0, part) + eb_ref[...]
    act_s[...] = (pre * mask[...]).astype(BF16)
    pre_s[...] = pre
    act_rows = pl.ds(pl.multiple_of(t * chunk, 16), chunk)
    act_cols = pl.ds(pl.multiple_of(c * lat, lat), lat)
    act_recv = []
    for d in range(1, X):
        to = wrap(t + d, X)
        for swap in (0, 1):
            dev = L + swap * (1 - 2 * c)
            act_recv.append(go(remote(act_s, act_f.at[act_rows, act_cols], dev, to)))
    act_recv.append(go(remote(act_s, act_f.at[act_rows, act_cols], partner, t)))
    act_f[act_rows, act_cols] = act_s[...]
    pre_recv = []
    for d in range(1, X):
        pre_recv.append(go(remote(pre_s, pre_f.at[my_rows], L, wrap(t + d, X))))
    pre_f[my_rows, :] = pre
    for d in act_recv:
        d.wait_recv()

    T[...] = jnp.dot(act_f[...], WD[...], preferred_element_type=F32)

    flying = {}
    for s in range(1, depth + 1):
        for o in (0, 1):
            for way in (1, -1):
                first = 0 if way == 1 else 1
                h = first if o == 0 else 1 - first
                if s == 1 and h != first:
                    continue
                target = wrap(b + way * (depth + 1 - s), n)
                at = pl.ds(pl.multiple_of(target * block, 8), block)
                cols = pl.ds(h * half, half)
                w = 0 if way == 1 else 1
                if s > (1 if h == first else 2):
                    flying[way, s - 1, h].wait_recv()
                    T[at, cols] = T[at, cols] + RB[w, s - 2, :, cols]
                flying[way, s, h] = go(
                    remote(T.at[at, cols], RB.at[w, s - 1, :, cols], lat_of(a, wrap(b + way, n)), t)
                )
    q = T[my_block, :]
    for o in (0, 1):
        for way in (1, -1):
            flying[way, depth, (0 if way == 1 else 1) ^ o].wait_recv()
    q = q + RB[0, depth - 1] + RB[1, depth - 1]
    for j in range(n):
        Q[j] = q[:, j * 128 : (j + 1) * 128]
    q_recv = []
    for d in range(1, n):
        to = wrap(a + d, n)
        q_recv.append(go(remote(Q.at[to], RQ.at[d - 1], lat_of(to, b), t)))
    piece = Q[a]
    for d in range(1, n):
        q_recv[d - 1].wait_recv()
        piece = piece + RQ[d - 1]
    a_cols = pl.ds(pl.multiple_of(a * 128, 128), 128)
    db_cols = pl.ds(pl.multiple_of(c * width + a * 128, 128), 128)
    piece = piece + db_ref[:, db_cols] - XF[c, my_block, a_cols].astype(F32)
    RES[my_block, a_cols] = piece.astype(BF16)

    r_recv = []
    for d in range(1, n):
        to = wrap(a + d, n)
        r_recv.append(go(remote(RES.at[my_block, a_cols], RES.at[my_block, a_cols], lat_of(to, b), t)))
    for d in r_recv:
        d.wait_recv()
    ring_gather(RES)

    r_swap = go(remote(RES, RESF, partner, t))
    part = lax.dot_general(RES[...], WD[...], nt, preferred_element_type=F32)
    back = feature_sum(1, part)
    ag_s[...] = (0.5 * back * mask[...]).astype(BF16)
    ag_recv = []
    for d in range(1, X):
        ag_recv.append(go(remote(ag_s, ag_f.at[act_rows], L, wrap(t + d, X))))
    ag_f[act_rows, :] = ag_s[...]

    r_swap.wait_recv()
    x_swap.wait_recv()
    acts = act_f[:, act_cols]
    near = RES[...]
    far = RESF[...]
    near_g = (0.5 * lax.dot_general(acts, near, tn, preferred_element_type=F32)).astype(BF16)
    far_g = (0.5 * lax.dot_general(acts, far, tn, preferred_element_type=F32)).astype(BF16)
    gd_out[:, own_cols] = near_g
    gd_out[:, far_cols] = far_g
    pick_i = lax.broadcasted_iota(jnp.int32, (16, rows), 0)
    pick_j = lax.broadcasted_iota(jnp.int32, (16, rows), 1)
    pick = jnp.where((pick_i < own) & (pick_j == pick_i + L * own), 1.0, 0.0).astype(BF16)
    res_out[:, own_cols] = jnp.dot(pick, near, preferred_element_type=F32)[:own].astype(BF16)
    res_out[:, far_cols] = jnp.dot(pick, far, preferred_element_type=F32)[:own].astype(BF16)
    for d in pre_recv:
        d.wait_recv()
    pre_out[...] = pre_f[...]

    for d in ag_recv:
        d.wait_recv()
    grads = ag_f[...]
    for h in (0, 1):
        ge_out[:, h * width : (h + 1) * width] = lax.dot_general(
            grads, XF[h], tn, preferred_element_type=F32
        ).astype(BF16)
    for d in sends:
        d.wait_send()


def shards(mesh, resid_stream, enc_weight, enc_bias, dec_weight, dec_bias, active_ids, active_count):
    own, width = resid_stream.shape
    lat = enc_weight.shape[0]
    dm = Dims(mesh, own, width, lat, active_ids.shape[1])
    n, rows, block, w = dm.n, dm.rows, dm.block, dm.width
    vmem = pl.BlockSpec(memory_space=pltpu.VMEM)
    hbm = pl.BlockSpec(memory_space=pl.ANY)
    copies = 160
    out = pl.pallas_call(
        functools.partial(kernel, dm),
        out_shape=(
            jax.ShapeDtypeStruct((rows, lat), F32),
            jax.ShapeDtypeStruct((own, width), BF16),
            jax.ShapeDtypeStruct((lat, width), BF16),
            jax.ShapeDtypeStruct((lat, width), BF16),
        ),
        in_specs=[vmem] * 5 + [hbm] * 2,
        out_specs=(vmem,) * 4,
        scratch_shapes=[
            pltpu.VMEM((2, dm.flat, 128), F32),
            pltpu.VMEM((2 * n * dm.flat, 128), F32),
            pltpu.VMEM((rows, w), BF16),
            pltpu.VMEM((2, rows, w), BF16),
            pltpu.VMEM((2 * lat, w), BF16),
            pltpu.VMEM((2 * lat, w), BF16),
            pltpu.VMEM((2, 2, rows, lat), F32),
            pltpu.VMEM((2, rows, lat), F32),
            pltpu.VMEM((2, rows, lat), F32),
            pltpu.VMEM((2, dm.X - 1, dm.chunk, lat), F32),
            pltpu.VMEM((dm.chunk, lat), F32),
            pltpu.VMEM((dm.chunk, lat), BF16),
            pltpu.VMEM((rows, 2 * lat), BF16),
            pltpu.VMEM((dm.chunk, lat), F32),
            pltpu.VMEM((rows, lat), F32),
            pltpu.VMEM((rows, w), F32),
            pltpu.VMEM((2, n // 2, block, w), F32),
            pltpu.VMEM((n, block, 128), F32),
            pltpu.VMEM((n - 1, block, 128), F32),
            pltpu.VMEM((rows, w), BF16),
            pltpu.VMEM((rows, w), BF16),
            pltpu.VMEM((dm.chunk, lat), BF16),
            pltpu.VMEM((rows, lat), BF16),
            pltpu.SemaphoreType.DMA((copies,)),
            pltpu.SemaphoreType.DMA((copies,)),
            pltpu.SemaphoreType.DMA((4,)),
        ],
        compiler_params=pltpu.CompilerParams(
            collective_id=0, has_side_effects=True, vmem_limit_bytes=48 * 1024 * 1024
        ),
    )(
        resid_stream,
        active_ids,
        active_count.reshape(1, rows),
        enc_bias.reshape(1, lat),
        dec_bias.reshape(1, width),
        enc_weight,
        dec_weight,
    )
    return tuple(out)


def solution(mesh):
    placed = (P("lat", "tok"), P("lat", "tok"), P("lat"), P("lat", "tok"), P("tok"), P(), P())
    return jax.shard_map(
        functools.partial(shards, mesh),
        mesh=mesh,
        in_specs=placed,
        out_specs=(P(None, "lat"), P("lat", "tok"), P("lat", "tok"), P("lat", "tok")),
        check_vma=False,
    )
```

```python
import functools
import math

import jax
import jax.numpy as jnp
from jax import lax
from jax.experimental import pallas as pl
from jax.experimental.pallas import tpu as pltpu
from jax.sharding import PartitionSpec as P

F32 = jnp.float32
BF16 = jnp.bfloat16
MESH = pl.DeviceIdType.MESH


def divisor(limit, by):
    s = 16
    m = (1 << s) // by + 1
    assert all((i * m) >> s == i // by for i in range(limit))
    return m, s


class Dims:
    def __init__(self, mesh, rows_own, width, lat_dev, top_count):
        self.X = mesh.shape["tok"]
        self.n = math.isqrt(mesh.shape["lat"] // 2)
        assert self.n * self.n * 2 == mesh.shape["lat"]
        self.own = rows_own
        self.rows = rows_own * mesh.shape["lat"]
        self.block = self.rows // self.n
        self.width = width // 2
        self.lanes = self.width // 128
        self.flat = rows_own * self.lanes
        self.lat = lat_dev
        self.top = top_count
        self.chunk = self.rows // self.X
        self.parts = 4
        self.part_cols = self.width // self.parts


def kernel(
    dm,
    x_hbm, ids_hbm, cnt_hbm, eb_hbm, db_hbm, enc_ref, dec_ref,
    pre_f, res_out, gd_out, ag_f, XF,
    xs, ids_ref, cnt_ref, eb_ref, db_ref, F, R1, Xraw, WE, WD, PS, PR, SUM, RX, mask_all, mask, act_s, act_f, pre_s,
    T, RB, Q, RQ, RES, RESF, ag_s,
    send, recv, local,
):
    n, X, own, block, width, lanes, flat = dm.n, dm.X, dm.own, dm.block, dm.width, dm.lanes, dm.flat
    rows, lat, chunk = dm.rows, dm.lat, dm.chunk
    parts, part_cols = dm.parts, dm.part_cols
    depth = n // 2
    L = lax.axis_index("lat")
    t = lax.axis_index("tok")
    c = lax.rem(L, 2)
    chip = L // 2
    y = lax.rem(chip, n)
    z = chip // n
    a = y + c * (z - y)
    b = z + c * (y - z)
    partner = L + 1 - 2 * c

    def lat_of(ap, bp):
        yy = ap + c * (bp - ap)
        zz = bp + c * (ap - bp)
        return (zz * n + yy) * 2 + c

    count = {"copy": 0, "local": 0}
    sends = []

    def wrap(v, m):
        return lax.rem(v + 2 * m, m)

    def remote(src, dst, lat_id, tok_id, recv_index=None):
        k = count["copy"]
        count["copy"] += 1
        r = k if recv_index is None else recv_index
        d = pltpu.make_async_remote_copy(
            src_ref=src, dst_ref=dst, send_sem=send.at[k], recv_sem=recv.at[r],
            device_id=(lat_id, tok_id), device_id_type=MESH,
        )
        return d

    def go(d):
        d.start()
        sends.append(d)
        return d

    def copy_local(src, dst):
        k = count["local"]
        count["local"] += 1
        d = pltpu.make_async_copy(src, dst, local.at[k])
        d.start()
        return d

    x_in = copy_local(x_hbm, xs)

    barrier = pltpu.get_barrier_semaphore()
    heard = 0

    def greet(lat_id, tok_id):
        pl.semaphore_signal(barrier, inc=1, device_id=(lat_id, tok_id), device_id_type=MESH)

    greet(partner, t)
    heard += 1
    for d in range(1, n):
        for other in (0, 1):
            dev = lat_of(wrap(a + d, n), b)
            greet(dev + other * (1 - 2 * c), t)
    heard += 2 * (n - 1)
    for s in (1, -1):
        greet(lat_of(a, wrap(b + s, n)), t)
    heard += 2
    for d in range(1, X):
        for dev in (L, partner):
            greet(dev, wrap(t + d, X))
    heard += 2 * (X - 1)

    x_in.wait()
    xv = xs[...].astype(F32)
    for r in range(own):
        for j in range(2 * lanes):
            F[j // lanes, r * lanes + j % lanes : r * lanes + j % lanes + 1, :] = xv[
                r : r + 1, j * 128 : (j + 1) * 128
            ]

    small_in = [
        copy_local(ids_hbm, ids_ref),
        copy_local(cnt_hbm, cnt_ref),
        copy_local(eb_hbm, eb_ref),
        copy_local(db_hbm, db_ref),
    ]
    pl.semaphore_wait(barrier, heard)

    recv1 = count["copy"]
    count["copy"] += 2 * n

    def slot1(pos, core):
        return pl.ds(pl.multiple_of((pos * 2 + core) * flat, 8), flat)

    go(remote(F.at[1 - c], R1.at[slot1(y + (1 - c) * (z - y), c)], partner, t, recv1 + c))
    for d in range(1, n):
        for h in (0, 1):
            pos = (y, z)[h]
            yy = wrap(y + d, n) if h == 0 else y
            zz = wrap(z + d, n) if h == 1 else z
            go(remote(F.at[h], R1.at[slot1(pos, c)], (zz * n + yy) * 2 + h, t, recv1 + 2 * d + c))
    mine = F[c]
    R1[slot1(a, c), :] = mine

    own_cols = pl.ds(pl.multiple_of(c * width, 128), width)
    far_cols = pl.ds(pl.multiple_of((1 - c) * width, 128), width)
    own_lats = pl.ds(pl.multiple_of(c * lat, lat), lat)
    w_local = [copy_local(enc_ref.at[:, own_cols], WE.at[own_lats]), copy_local(dec_ref.at[:, own_cols], WD.at[own_lats])]
    w_remote = [
        go(remote(enc_ref.at[:, far_cols], WE.at[own_lats], partner, t)),
        go(remote(dec_ref.at[:, far_cols], WD.at[own_lats], partner, t)),
    ]

    my_rows = pl.ds(pl.multiple_of(t * chunk, 8), chunk)
    for d in small_in:
        d.wait()
    k_i = lax.broadcasted_iota(jnp.int32, (dm.top, rows), 0)
    local_ids = jnp.where(k_i < jnp.broadcast_to(cnt_ref[...].reshape(1, rows), (dm.top, rows)), ids_ref[...] - L * lat, -1)
    lat_i = lax.broadcasted_iota(jnp.int32, (lat, rows), 0)
    m = jnp.zeros((lat, rows), F32)
    for k in range(dm.top):
        m = jnp.where(local_ids[k : k + 1, :] == lat_i, 1.0, m)
    mask_all[...] = m.T
    mask[...] = mask_all[my_rows, :]

    m1, s1 = divisor(rows, block)
    m2, s2 = divisor(block, block // n)
    i0 = lax.broadcasted_iota(jnp.int32, (rows, rows), 0)
    i1 = lax.broadcasted_iota(jnp.int32, (rows, rows), 1)
    hi = (i0 * m1) >> s1
    rest = i0 - hi * block
    mid = (rest * m2) >> s2
    low = rest - mid * (block // n)
    order = i0 + c * (mid * block + hi * (block // n) + low - i0)
    perm = jnp.where(order == i1, 1.0, 0.0).astype(BF16)

    def remote_wait(index):
        pltpu.make_async_remote_copy(
            src_ref=F.at[0], dst_ref=R1.at[pl.ds(0, flat)], send_sem=send.at[0], recv_sem=recv.at[index],
            device_id=(partner, t), device_id_type=MESH,
        ).wait_recv()

    remote_wait(recv1 + 1 - c)
    for d in range(1, n):
        for core in (0, 1):
            remote_wait(recv1 + 2 * d + core)
    my_block = pl.ds(pl.multiple_of(b * block, 16), block)
    for j in range(lanes):
        at = j * 128 % part_cols
        Xraw[j * 128 // part_cols, my_block, at : at + 128] = R1[pl.ds(j, block, stride=lanes), :].astype(BF16)

    def far_parts(way):
        return range(parts // 2) if way == 1 else range(parts // 2, parts)

    def near_parts(way):
        return far_parts(-way)

    def block_rows(pos):
        return pl.ds(pl.multiple_of(pos * block, 16), block)

    def ring_gather(buf):
        flying = {}
        for s in range(1, depth + 1):
            for i in range(parts):
                for way in (1, -1):
                    h = (*far_parts(way), *near_parts(way))[i]
                    if s > 1:
                        flying[way, s - 1, h].wait_recv()
                    if s < depth or h in far_parts(way):
                        piece = buf.at[h, block_rows(wrap(b - way * (s - 1), n))]
                        flying[way, s, h] = go(remote(piece, piece, lat_of(a, wrap(b + way, n)), t))
        for i in range(parts // 2):
            for way in (1, -1):
                flying[way, depth, far_parts(way)[i]].wait_recv()

    ring_gather(Xraw)

    for w in w_local:
        w.wait()
    for w in w_remote:
        w.wait_recv()

    for h in range(parts):
        XF[c, :, h * part_cols : (h + 1) * part_cols] = jnp.dot(perm, Xraw[h], preferred_element_type=F32).astype(BF16)
    x_swap = go(remote(XF.at[c], XF.at[c], partner, t))

    order = sorted(range(X), key=lambda d: -min(d, X - d))

    def feature_sum(u, lhs, rhs):
        swap = {}
        arrive = {}
        for d in order:
            part = lax.dot_general(
                lhs(pl.ds(pl.multiple_of(wrap(t + d, X) * chunk, 16), chunk)), rhs, nt, preferred_element_type=F32
            )
            PS[u, d, 0] = part[:, :lat]
            PS[u, d, 1] = part[:, lat:]
            swap[d] = go(remote(PS.at[u, d, 1 - c], PR.at[u, d], partner, t))
        for d in order:
            swap[d].wait_recv()
            SUM[u, d] = PS[u, d, c] + PR[u, d]
            if d:
                arrive[d] = go(remote(SUM.at[u, d], RX.at[u, d - 1], L, wrap(t + d, X)))
        total = SUM[u, 0]
        for d in sorted(arrive, key=lambda d: min(d, X - d)):
            arrive[d].wait_recv()
            total = total + RX[u, d - 1]
        return total

    nt = (((1,), (1,)), ((), ()))
    tn = (((0,), (0,)), ((), ()))
    pre = feature_sum(0, lambda r: XF[c, r, :], WE[...]) + eb_ref[...]
    act_s[...] = (pre * mask[...]).astype(BF16)
    pre_s[...] = pre
    act_rows = pl.ds(pl.multiple_of(t * chunk, 16), chunk)
    act_cols = pl.ds(pl.multiple_of(c * lat, lat), lat)
    act_recv = []
    for d in range(1, X):
        to = wrap(t + d, X)
        for swap in (0, 1):
            dev = L + swap * (1 - 2 * c)
            act_recv.append(go(remote(act_s, act_f.at[act_rows, act_cols], dev, to)))
    act_recv.append(go(remote(act_s, act_f.at[act_rows, act_cols], partner, t)))
    act_f[act_rows, act_cols] = act_s[...]
    pre_recv = []
    for d in range(1, X):
        pre_recv.append(go(remote(pre_s, pre_f.at[my_rows], L, wrap(t + d, X))))
    pre_f[my_rows, :] = pre
    for d in act_recv:
        d.wait_recv()

    def rebuild(pos):
        at = block_rows(pos)
        value = jnp.dot(act_f[at, :], WD[...], preferred_element_type=F32)
        for h in range(parts):
            T[h, at, :] = value[:, h * part_cols : (h + 1) * part_cols]

    flying = {}

    def ring_reduce_hop(i):
        for k in range(parts):
            for way in (1, -1):
                far = k < parts // 2
                h = (*far_parts(way), *near_parts(way))[k]
                hops = depth if far else depth - 1
                if i > hops:
                    continue
                at = block_rows(wrap(b + way * (hops + 1 - i), n))
                w = 0 if way == 1 else 1
                if i > 1:
                    flying[way, i - 1, h].wait_recv()
                    T[h, at, :] = T[h, at, :] + RB[w, i - 2, h]
                flying[way, i, h] = go(remote(T.at[h, at], RB.at[w, i - 1, h], lat_of(a, wrap(b + way, n)), t))

    rebuild(wrap(b + depth, n))
    for k in range(depth - 1, 0, -1):
        rebuild(wrap(b + k, n))
        rebuild(wrap(b - k, n))
        if k == depth - 1:
            ring_reduce_hop(1)
    rebuild(b)
    for i in range(2, depth + 1):
        ring_reduce_hop(i)
    for h in (*near_parts(1), *far_parts(1)):
        q = T[h, my_block, :]
        for way in (1, -1):
            hops = depth if h in far_parts(way) else depth - 1
            flying[way, hops, h].wait_recv()
            q = q + RB[0 if way == 1 else 1, hops - 1, h]
        for j in range(part_cols // 128):
            Q[h * (part_cols // 128) + j] = q[:, j * 128 : (j + 1) * 128]
    q_recv = []
    for d in range(1, n):
        to = wrap(a + d, n)
        q_recv.append(go(remote(Q.at[to], RQ.at[d - 1], lat_of(to, b), t)))
    piece = Q[a]
    for d in range(1, n):
        q_recv[d - 1].wait_recv()
        piece = piece + RQ[d - 1]
    a_cols = pl.ds(pl.multiple_of(a * 128, 128), 128)
    db_cols = pl.ds(pl.multiple_of(c * width + a * 128, 128), 128)
    piece = piece + db_ref[:, db_cols] - XF[c, my_block, a_cols].astype(F32)
    per = part_cols // 128
    res_piece = RES.at[a // per, my_block, pl.ds(pl.multiple_of(lax.rem(a, per) * 128, 128), 128)]
    res_piece[...] = piece.astype(BF16)

    r_recv = []
    for d in range(1, n):
        to = wrap(a + d, n)
        r_recv.append(go(remote(res_piece, res_piece, lat_of(to, b), t)))
    for d in r_recv:
        d.wait_recv()
    ring_gather(RES)

    r_swap = go(remote(RES, RESF, partner, t))
    back = feature_sum(1, lambda r: jnp.concatenate([RES[h, r, :] for h in range(parts)], axis=1), WD[...])
    ag_s[...] = (0.5 * back * mask[...]).astype(BF16)
    ag_recv = []
    for d in range(1, X):
        ag_recv.append(go(remote(ag_s, ag_f.at[act_rows], L, wrap(t + d, X))))
    ag_f[act_rows, :] = ag_s[...]

    r_swap.wait_recv()
    x_swap.wait_recv()
    acts = act_f[:, act_cols]
    pick_i = lax.broadcasted_iota(jnp.int32, (16, rows), 0)
    pick_j = lax.broadcasted_iota(jnp.int32, (16, rows), 1)
    pick = jnp.where((pick_i < own) & (pick_j == pick_i + L * own), 1.0, 0.0).astype(BF16)
    for core, buf in ((c, RES), (1 - c, RESF)):
        for h in range(parts):
            cols = pl.ds(pl.multiple_of(core * width + h * part_cols, 128), part_cols)
            gd_out[:, cols] = (0.5 * lax.dot_general(acts, buf[h], tn, preferred_element_type=F32)).astype(BF16)
            res_out[:, cols] = jnp.dot(pick, buf[h], preferred_element_type=F32)[:own].astype(BF16)
    for d in pre_recv:
        d.wait_recv()
    for d in ag_recv:
        d.wait_recv()
    for d in sends:
        d.wait_send()


def finish(pre_ref, res_ref, gd_ref, ag_ref, xf_ref, pre_out, res_out, ge_out, gd_out, ge_s, sems):
    moves = [
        pltpu.make_async_copy(pre_ref, pre_out, sems.at[0]),
        pltpu.make_async_copy(res_ref, res_out, sems.at[1]),
        pltpu.make_async_copy(gd_ref, gd_out, sems.at[2]),
    ]
    for d in moves:
        d.start()
    width = ge_s.shape[2]
    grads = ag_ref[...]
    for h in (0, 1):
        ge_s[h] = lax.dot_general(
            grads, xf_ref[h], (((0,), (0,)), ((), ())), preferred_element_type=F32
        ).astype(BF16)
        d = pltpu.make_async_copy(ge_s.at[h], ge_out.at[:, pl.ds(h * width, width)], sems.at[3 + h])
        d.start()
        moves.append(d)
    for d in moves:
        d.wait()


def shards(mesh, resid_stream, enc_weight, enc_bias, dec_weight, dec_bias, active_ids, active_count):
    own, width = resid_stream.shape
    lat = enc_weight.shape[0]
    dm = Dims(mesh, own, width, lat, active_ids.shape[1])
    n, rows, block, w = dm.n, dm.rows, dm.block, dm.width
    vmem = pl.BlockSpec(memory_space=pltpu.VMEM)
    hbm = pl.BlockSpec(memory_space=pltpu.HBM)
    copies = 288
    pre, res, gd, ag, xf = pl.pallas_call(
        functools.partial(kernel, dm),
        out_shape=(
            jax.ShapeDtypeStruct((rows, lat), F32),
            jax.ShapeDtypeStruct((own, width), BF16),
            jax.ShapeDtypeStruct((lat, width), BF16),
            jax.ShapeDtypeStruct((rows, lat), BF16),
            jax.ShapeDtypeStruct((2, rows, w), BF16),
        ),
        in_specs=[hbm] * 7,
        out_specs=(vmem,) * 5,
        scratch_shapes=[
            pltpu.VMEM((own, width), BF16),
            pltpu.VMEM((dm.top, rows), jnp.int32),
            pltpu.VMEM((rows,), jnp.int32),
            pltpu.VMEM((1, lat), F32),
            pltpu.VMEM((1, width), F32),
            pltpu.VMEM((2, dm.flat, 128), F32),
            pltpu.VMEM((2 * n * dm.flat, 128), F32),
            pltpu.VMEM((dm.parts, rows, dm.part_cols), BF16),
            pltpu.VMEM((2 * lat, w), BF16),
            pltpu.VMEM((2 * lat, w), BF16),
            pltpu.VMEM((2, dm.X, 2, dm.chunk, lat), F32),
            pltpu.VMEM((2, dm.X, dm.chunk, lat), F32),
            pltpu.VMEM((2, dm.X, dm.chunk, lat), F32),
            pltpu.VMEM((2, dm.X - 1, dm.chunk, lat), F32),
            pltpu.VMEM((rows, lat), F32),
            pltpu.VMEM((dm.chunk, lat), F32),
            pltpu.VMEM((dm.chunk, lat), BF16),
            pltpu.VMEM((rows, 2 * lat), BF16),
            pltpu.VMEM((dm.chunk, lat), F32),
            pltpu.VMEM((dm.parts, rows, dm.part_cols), F32),
            pltpu.VMEM((2, n // 2, dm.parts, block, dm.part_cols), F32),
            pltpu.VMEM((n, block, 128), F32),
            pltpu.VMEM((n - 1, block, 128), F32),
            pltpu.VMEM((dm.parts, rows, dm.part_cols), BF16),
            pltpu.VMEM((dm.parts, rows, dm.part_cols), BF16),
            pltpu.VMEM((dm.chunk, lat), BF16),
            pltpu.SemaphoreType.DMA((copies,)),
            pltpu.SemaphoreType.DMA((copies,)),
            pltpu.SemaphoreType.DMA((8,)),
        ],
        compiler_params=pltpu.CompilerParams(
            collective_id=0, has_side_effects=True, vmem_limit_bytes=48 * 1024 * 1024
        ),
    )(
        *(
            pltpu.with_memory_space_constraint(v, pltpu.HBM)
            for v in (
                resid_stream,
                active_ids.T,
                active_count,
                enc_bias.reshape(1, lat),
                dec_bias.reshape(1, width),
                enc_weight,
                dec_weight,
            )
        )
    )
    return pl.pallas_call(
        finish,
        out_shape=(
            jax.ShapeDtypeStruct((rows, lat), F32),
            jax.ShapeDtypeStruct((own, width), BF16),
            jax.ShapeDtypeStruct((lat, width), BF16),
            jax.ShapeDtypeStruct((lat, width), BF16),
        ),
        in_specs=[vmem] * 5,
        out_specs=(hbm,) * 4,
        scratch_shapes=[pltpu.VMEM((2, lat, w), BF16), pltpu.SemaphoreType.DMA((5,))],
        compiler_params=pltpu.CompilerParams(vmem_limit_bytes=4 * 1024 * 1024),
    )(pre, res, gd, ag, xf)


def solution(mesh):
    placed = (P("lat", "tok"), P("lat", "tok"), P("lat"), P("lat", "tok"), P("tok"), P(), P())
    return jax.shard_map(
        functools.partial(shards, mesh),
        mesh=mesh,
        in_specs=placed,
        out_specs=(P(None, "lat"), P("lat", "tok"), P("lat", "tok"), P("lat", "tok")),
        check_vma=False,
    )
```

```python
import functools
import math

import jax
import jax.numpy as jnp
from jax import lax
from jax.experimental import pallas as pl
from jax.experimental.pallas import tpu as pltpu
from jax.sharding import PartitionSpec as P

F32 = jnp.float32
BF16 = jnp.bfloat16
MESH = pl.DeviceIdType.MESH


class Dims:
    def __init__(self, mesh, rows_own, width, lat_dev, top_count):
        self.X = mesh.shape["tok"]
        self.n = math.isqrt(mesh.shape["lat"] // 2)
        assert self.n == 8 and self.n * self.n * 2 == mesh.shape["lat"]
        self.own = rows_own
        self.rows = rows_own * mesh.shape["lat"]
        self.block = self.rows // self.n
        self.width = width // 2
        self.lanes = self.width // 128
        self.flat = rows_own * self.lanes
        self.lat = lat_dev
        self.top = top_count
        self.chunk = self.rows // self.X
        self.parts = 4
        self.part_cols = self.width // self.parts


def kernel(
    dm,
    x_hbm, ids_hbm, cnt_hbm, eb_hbm, db_hbm, enc_ref, dec_ref,
    pre_f, res_out, gd_out, ag_f, XF,
    xs, ids_ref, cnt_ref, eb_ref, db_ref, F32S, F, X3, XL, WE, WD, PS, PR, SUM, RX, mask_all, mask, act_s, act_f, pre_s,
    T, RB, Q, RQ, RES, RESF, ag_s,
    send, recv, local,
):
    n, X, own, block, width, lanes, flat = dm.n, dm.X, dm.own, dm.block, dm.width, dm.lanes, dm.flat
    rows, lat, chunk = dm.rows, dm.lat, dm.chunk
    parts, part_cols = dm.parts, dm.part_cols
    depth = n // 2
    L = lax.axis_index("lat")
    t = lax.axis_index("tok")
    c = lax.rem(L, 2)
    chip = L // 2
    y = lax.rem(chip, n)
    z = chip // n
    a = y + c * (z - y)
    b = z + c * (y - z)
    partner = L + 1 - 2 * c

    def lat_of(ap, bp):
        yy = ap + c * (bp - ap)
        zz = bp + c * (ap - bp)
        return (zz * n + yy) * 2 + c

    count = {"copy": 0, "local": 0}
    sends = []

    def wrap(v, m):
        return lax.rem(v + 2 * m, m)

    def remote(src, dst, lat_id, tok_id, recv_index=None):
        k = count["copy"]
        count["copy"] += 1
        r = k if recv_index is None else recv_index
        d = pltpu.make_async_remote_copy(
            src_ref=src, dst_ref=dst, send_sem=send.at[k], recv_sem=recv.at[r],
            device_id=(lat_id, tok_id), device_id_type=MESH,
        )
        return d

    def go(d):
        d.start()
        sends.append(d)
        return d

    def copy_local(src, dst):
        k = count["local"]
        count["local"] += 1
        d = pltpu.make_async_copy(src, dst, local.at[k])
        d.start()
        return d

    x_in = copy_local(x_hbm, xs)

    barrier = pltpu.get_barrier_semaphore()
    heard = 0

    def greet(lat_id, tok_id):
        pl.semaphore_signal(barrier, inc=1, device_id=(lat_id, tok_id), device_id_type=MESH)

    greet(partner, t)
    heard += 1
    for d in range(1, n):
        for other in (0, 1):
            dev = lat_of(wrap(a + d, n), b)
            greet(dev + other * (1 - 2 * c), t)
    heard += 2 * (n - 1)
    for s in (1, -1, 2, -2):
        greet(lat_of(a, wrap(b + s, n)), t)
    heard += 4
    for d in range(1, X):
        for dev in (L, partner):
            greet(dev, wrap(t + d, X))
    heard += 2 * (X - 1)

    x_in.wait()
    xv = xs[...].astype(F32)
    for r in range(own):
        for j in range(2 * lanes):
            at = r * lanes + j % lanes
            F32S[j // lanes, at : at + 1, :] = xv[r : r + 1, j * 128 : (j + 1) * 128]
    for h in (0, 1):
        F[h] = F32S[h].reshape(own, lanes, 128).astype(BF16)

    small_in = [
        copy_local(ids_hbm, ids_ref),
        copy_local(cnt_hbm, cnt_ref),
        copy_local(eb_hbm, eb_ref),
        copy_local(db_hbm, db_ref),
    ]
    pl.semaphore_wait(barrier, heard)

    recv1 = count["copy"]
    count["copy"] += 2 * n

    my_x = X3.at[pl.ds(L * own, own)]
    go(remote(F.at[1 - c], my_x, partner, t, recv1 + c))
    for d in range(1, n):
        for h in (0, 1):
            yy = wrap(y + d, n) if h == 0 else y
            zz = wrap(z + d, n) if h == 1 else z
            go(remote(F.at[h], my_x, (zz * n + yy) * 2 + h, t, recv1 + 2 * d + c))
    my_x[...] = F[c]

    own_cols = pl.ds(pl.multiple_of(c * width, 128), width)
    far_cols = pl.ds(pl.multiple_of((1 - c) * width, 128), width)
    own_lats = pl.ds(pl.multiple_of(c * lat, lat), lat)
    w_local = [copy_local(enc_ref.at[:, own_cols], WE.at[own_lats]), copy_local(dec_ref.at[:, own_cols], WD.at[own_lats])]
    w_remote = [
        go(remote(enc_ref.at[:, far_cols], WE.at[own_lats], partner, t)),
        go(remote(dec_ref.at[:, far_cols], WD.at[own_lats], partner, t)),
    ]

    my_rows = pl.ds(pl.multiple_of(t * chunk, 8), chunk)
    for d in small_in:
        d.wait()
    k_i = lax.broadcasted_iota(jnp.int32, (dm.top, rows), 0)
    local_ids = jnp.where(k_i < jnp.broadcast_to(cnt_ref[...].reshape(1, rows), (dm.top, rows)), ids_ref[...] - L * lat, -1)
    lat_i = lax.broadcasted_iota(jnp.int32, (lat, rows), 0)
    m = jnp.zeros((lat, rows), F32)
    for k in range(dm.top):
        m = jnp.where(local_ids[k : k + 1, :] == lat_i, 1.0, m)
    mask_all[...] = m.T
    mask[...] = mask_all[my_rows, :]

    def far_parts(way):
        return range(parts // 2) if way == 1 else range(parts // 2, parts)

    def near_parts(way):
        return far_parts(-way)

    def block_rows(pos):
        return pl.ds(pl.multiple_of(pos * block, 16), block)

    my_block = block_rows(b)

    def spread(piece, ready):
        by_distance = sorted(range(n), key=lambda d: min(d, n - d))
        first, second = {}, {}

        def push(offset, d, pos):
            ref = piece(wrap(a + d, n), wrap(pos, n))
            return go(remote(ref, ref, lat_of(a, wrap(b + offset, n)), t))

        def level1(d):
            ready(d)
            for offset in (2, -2, 1, -1):
                first[offset, d] = push(offset, d, b)

        def level2(k, d):
            for way in (1, -1):
                first[2 * way, d].wait_recv()
                if (k % 2 == 0) == (way == 1):
                    second[2 * way, d] = push(2 * way, d, b - 2 * way)
                second[way, d] = push(way, d, b - 2 * way)

        for d in by_distance[:5]:
            level1(d)
        level2(0, by_distance[0])
        for d in by_distance[5:]:
            level1(d)
        for k, d in enumerate(by_distance):
            if k:
                level2(k, d)
        for d in by_distance:
            first[1, d].wait_recv()
            first[-1, d].wait_recv()
        for got in second.values():
            got.wait_recv()

    def x_ready(d):
        back = (n - d) % n
        for core in (0, 1) if d else (1 - c,):
            pltpu.make_async_remote_copy(
                src_ref=F.at[0], dst_ref=X3.at[pl.ds(0, own)], send_sem=send.at[0],
                recv_sem=recv.at[recv1 + 2 * back + core], device_id=(partner, t), device_id_type=MESH,
            ).wait_recv()

    def x_piece(ap, bp):
        return X3.at[pl.ds((lat_of(ap, bp) - c) * own, 2 * own)]

    spread(x_piece, x_ready)

    for w in w_local:
        w.wait()
    for w in w_remote:
        w.wait_recv()

    XL[...] = X3[...].astype(F32).reshape(rows * lanes, 128)
    for j in range(lanes):
        XF[c, :, j * 128 : (j + 1) * 128] = XL[pl.ds(j, rows, stride=lanes), :].astype(BF16)
    x_swap = go(remote(XF.at[c], XF.at[c], partner, t))

    order = sorted(range(X), key=lambda d: -min(d, X - d))

    def feature_sum(u, lhs, rhs):
        swap = {}
        arrive = {}
        for d in order:
            part = lax.dot_general(
                lhs(pl.ds(pl.multiple_of(wrap(t + d, X) * chunk, 16), chunk)), rhs, nt, preferred_element_type=F32
            )
            PS[u, d, 0] = part[:, :lat]
            PS[u, d, 1] = part[:, lat:]
            swap[d] = go(remote(PS.at[u, d, 1 - c], PR.at[u, d], partner, t))
        for d in order:
            swap[d].wait_recv()
            SUM[u, d] = PS[u, d, c] + PR[u, d]
            if d:
                arrive[d] = go(remote(SUM.at[u, d], RX.at[u, d - 1], L, wrap(t + d, X)))
        total = SUM[u, 0]
        for d in sorted(arrive, key=lambda d: min(d, X - d)):
            arrive[d].wait_recv()
            total = total + RX[u, d - 1]
        return total

    nt = (((1,), (1,)), ((), ()))
    tn = (((0,), (0,)), ((), ()))
    pre = feature_sum(0, lambda r: XF[c, r, :], WE[...]) + eb_ref[...]
    act_s[...] = (pre * mask[...]).astype(BF16)
    pre_s[...] = pre
    act_rows = pl.ds(pl.multiple_of(t * chunk, 16), chunk)
    act_cols = pl.ds(pl.multiple_of(c * lat, lat), lat)
    act_recv = []
    for d in range(1, X):
        to = wrap(t + d, X)
        for swap in (0, 1):
            dev = L + swap * (1 - 2 * c)
            act_recv.append(go(remote(act_s, act_f.at[act_rows, act_cols], dev, to)))
    act_recv.append(go(remote(act_s, act_f.at[act_rows, act_cols], partner, t)))
    act_f[act_rows, act_cols] = act_s[...]
    pre_recv = []
    for d in range(1, X):
        pre_recv.append(go(remote(pre_s, pre_f.at[my_rows], L, wrap(t + d, X))))
    pre_f[my_rows, :] = pre
    for d in act_recv:
        d.wait_recv()

    def rebuild(pos):
        at = block_rows(pos)
        value = jnp.dot(act_f[at, :], WD[...], preferred_element_type=F32)
        for h in range(parts):
            T[h, at, :] = value[:, h * part_cols : (h + 1) * part_cols]

    flying = {}

    def ring_reduce_hop(i):
        for k in range(parts):
            for way in (1, -1):
                far = k < parts // 2
                h = (*far_parts(way), *near_parts(way))[k]
                hops = depth if far else depth - 1
                if i > hops:
                    continue
                at = block_rows(wrap(b + way * (hops + 1 - i), n))
                w = 0 if way == 1 else 1
                if i > 1:
                    flying[way, i - 1, h].wait_recv()
                    T[h, at, :] = T[h, at, :] + RB[w, i - 2, h]
                flying[way, i, h] = go(remote(T.at[h, at], RB.at[w, i - 1, h], lat_of(a, wrap(b + way, n)), t))

    rebuild(wrap(b + depth, n))
    for k in range(depth - 1, 0, -1):
        rebuild(wrap(b + k, n))
        rebuild(wrap(b - k, n))
        if k == depth - 1:
            ring_reduce_hop(1)
    rebuild(b)
    for i in range(2, depth + 1):
        ring_reduce_hop(i)
    for h in (*near_parts(1), *far_parts(1)):
        q = T[h, my_block, :]
        for way in (1, -1):
            hops = depth if h in far_parts(way) else depth - 1
            flying[way, hops, h].wait_recv()
            q = q + RB[0 if way == 1 else 1, hops - 1, h]
        for j in range(part_cols // 128):
            Q[h * (part_cols // 128) + j] = q[:, j * 128 : (j + 1) * 128]
    q_recv = []
    for d in range(1, n):
        to = wrap(a + d, n)
        q_recv.append(go(remote(Q.at[to], RQ.at[d - 1], lat_of(to, b), t)))
    piece = Q[a]
    for d in range(1, n):
        q_recv[d - 1].wait_recv()
        piece = piece + RQ[d - 1]
    a_cols = pl.ds(pl.multiple_of(a * 128, 128), 128)
    db_cols = pl.ds(pl.multiple_of(c * width + a * 128, 128), 128)
    piece = piece + db_ref[:, db_cols] - XF[c, my_block, a_cols].astype(F32)
    RES[a, my_block, :] = piece.astype(BF16)

    def res_piece(ap, bp):
        return RES.at[ap, block_rows(bp)]

    r_recv = {}
    for d in range(1, n):
        ref = res_piece(a, b)
        r_recv[n - d] = go(remote(ref, ref, lat_of(wrap(a + d, n), b), t))

    def res_ready(d):
        if d:
            r_recv[d].wait_recv()

    spread(res_piece, res_ready)

    r_swap = go(remote(RES, RESF, partner, t))
    back = feature_sum(1, lambda r: jnp.concatenate([RES[j, r, :] for j in range(lanes)], axis=1), WD[...])
    ag_s[...] = (0.5 * back * mask[...]).astype(BF16)
    ag_recv = []
    for d in range(1, X):
        ag_recv.append(go(remote(ag_s, ag_f.at[act_rows], L, wrap(t + d, X))))
    ag_f[act_rows, :] = ag_s[...]

    r_swap.wait_recv()
    x_swap.wait_recv()
    acts = act_f[:, act_cols]
    pick_i = lax.broadcasted_iota(jnp.int32, (16, rows), 0)
    pick_j = lax.broadcasted_iota(jnp.int32, (16, rows), 1)
    pick = jnp.where((pick_i < own) & (pick_j == pick_i + L * own), 1.0, 0.0).astype(BF16)
    for cols, buf in ((own_cols, RES), (far_cols, RESF)):
        value = jnp.concatenate([buf[j] for j in range(lanes)], axis=1)
        gd_out[:, cols] = (0.5 * lax.dot_general(acts, value, tn, preferred_element_type=F32)).astype(BF16)
        res_out[:, cols] = jnp.dot(pick, value, preferred_element_type=F32)[:own].astype(BF16)
    for d in pre_recv:
        d.wait_recv()
    for d in ag_recv:
        d.wait_recv()
    for d in sends:
        d.wait_send()


def finish(pre_ref, res_ref, gd_ref, ag_ref, xf_ref, pre_out, res_out, ge_out, gd_out, ge_s, sems):
    moves = [
        pltpu.make_async_copy(pre_ref, pre_out, sems.at[0]),
        pltpu.make_async_copy(res_ref, res_out, sems.at[1]),
        pltpu.make_async_copy(gd_ref, gd_out, sems.at[2]),
    ]
    for d in moves:
        d.start()
    width = ge_s.shape[2]
    grads = ag_ref[...]
    for h in (0, 1):
        ge_s[h] = lax.dot_general(
            grads, xf_ref[h], (((0,), (0,)), ((), ())), preferred_element_type=F32
        ).astype(BF16)
        d = pltpu.make_async_copy(ge_s.at[h], ge_out.at[:, pl.ds(h * width, width)], sems.at[3 + h])
        d.start()
        moves.append(d)
    for d in moves:
        d.wait()


def shards(mesh, resid_stream, enc_weight, enc_bias, dec_weight, dec_bias, active_ids, active_count):
    own, width = resid_stream.shape
    lat = enc_weight.shape[0]
    dm = Dims(mesh, own, width, lat, active_ids.shape[1])
    n, rows, block, w = dm.n, dm.rows, dm.block, dm.width
    vmem = pl.BlockSpec(memory_space=pltpu.VMEM)
    hbm = pl.BlockSpec(memory_space=pltpu.HBM)
    copies = 288
    pre, res, gd, ag, xf = pl.pallas_call(
        functools.partial(kernel, dm),
        out_shape=(
            jax.ShapeDtypeStruct((rows, lat), F32),
            jax.ShapeDtypeStruct((own, width), BF16),
            jax.ShapeDtypeStruct((lat, width), BF16),
            jax.ShapeDtypeStruct((rows, lat), BF16),
            jax.ShapeDtypeStruct((2, rows, w), BF16),
        ),
        in_specs=[hbm] * 7,
        out_specs=(vmem,) * 5,
        scratch_shapes=[
            pltpu.VMEM((own, width), BF16),
            pltpu.VMEM((dm.top, rows), jnp.int32),
            pltpu.VMEM((rows,), jnp.int32),
            pltpu.VMEM((1, lat), F32),
            pltpu.VMEM((1, width), F32),
            pltpu.VMEM((2, dm.flat, 128), F32),
            pltpu.VMEM((2, own, dm.lanes, 128), BF16),
            pltpu.VMEM((rows, dm.lanes, 128), BF16),
            pltpu.VMEM((rows * dm.lanes, 128), F32),
            pltpu.VMEM((2 * lat, w), BF16),
            pltpu.VMEM((2 * lat, w), BF16),
            pltpu.VMEM((2, dm.X, 2, dm.chunk, lat), F32),
            pltpu.VMEM((2, dm.X, dm.chunk, lat), F32),
            pltpu.VMEM((2, dm.X, dm.chunk, lat), F32),
            pltpu.VMEM((2, dm.X - 1, dm.chunk, lat), F32),
            pltpu.VMEM((rows, lat), F32),
            pltpu.VMEM((dm.chunk, lat), F32),
            pltpu.VMEM((dm.chunk, lat), BF16),
            pltpu.VMEM((rows, 2 * lat), BF16),
            pltpu.VMEM((dm.chunk, lat), F32),
            pltpu.VMEM((dm.parts, rows, dm.part_cols), F32),
            pltpu.VMEM((2, n // 2, dm.parts, block, dm.part_cols), F32),
            pltpu.VMEM((n, block, 128), F32),
            pltpu.VMEM((n - 1, block, 128), F32),
            pltpu.VMEM((dm.lanes, rows, 128), BF16),
            pltpu.VMEM((dm.lanes, rows, 128), BF16),
            pltpu.VMEM((dm.chunk, lat), BF16),
            pltpu.SemaphoreType.DMA((copies,)),
            pltpu.SemaphoreType.DMA((copies,)),
            pltpu.SemaphoreType.DMA((8,)),
        ],
        compiler_params=pltpu.CompilerParams(
            collective_id=0, has_side_effects=True, vmem_limit_bytes=48 * 1024 * 1024
        ),
    )(
        *(
            pltpu.with_memory_space_constraint(v, pltpu.HBM)
            for v in (
                resid_stream,
                active_ids.T,
                active_count,
                enc_bias.reshape(1, lat),
                dec_bias.reshape(1, width),
                enc_weight,
                dec_weight,
            )
        )
    )
    return pl.pallas_call(
        finish,
        out_shape=(
            jax.ShapeDtypeStruct((rows, lat), F32),
            jax.ShapeDtypeStruct((own, width), BF16),
            jax.ShapeDtypeStruct((lat, width), BF16),
            jax.ShapeDtypeStruct((lat, width), BF16),
        ),
        in_specs=[vmem] * 5,
        out_specs=(hbm,) * 4,
        scratch_shapes=[pltpu.VMEM((2, lat, w), BF16), pltpu.SemaphoreType.DMA((5,))],
        compiler_params=pltpu.CompilerParams(vmem_limit_bytes=4 * 1024 * 1024),
    )(pre, res, gd, ag, xf)


def solution(mesh):
    placed = (P("lat", "tok"), P("lat", "tok"), P("lat"), P("lat", "tok"), P("tok"), P(), P())
    return jax.shard_map(
        functools.partial(shards, mesh),
        mesh=mesh,
        in_specs=placed,
        out_specs=(P(None, "lat"), P("lat", "tok"), P("lat", "tok"), P("lat", "tok")),
        check_vma=False,
    )
```

```python
import functools
import math

import jax
import jax.numpy as jnp
from jax import lax
from jax.experimental import pallas as pl
from jax.experimental.pallas import tpu as pltpu
from jax.sharding import PartitionSpec as P

F32 = jnp.float32
BF16 = jnp.bfloat16
MESH = pl.DeviceIdType.MESH


class Dims:
    def __init__(self, mesh, rows_own, width, lat_dev, top_count):
        self.X = mesh.shape["tok"]
        self.n = math.isqrt(mesh.shape["lat"] // 2)
        assert self.n == 8 and self.n * self.n * 2 == mesh.shape["lat"]
        self.own = rows_own
        self.rows = rows_own * mesh.shape["lat"]
        self.block = self.rows // self.n
        self.width = width // 2
        self.lanes = self.width // 128
        self.flat = rows_own * self.lanes
        self.lat = lat_dev
        self.top = top_count
        self.chunk = self.rows // self.X


def kernel(
    dm,
    x_hbm, ids_hbm, cnt_hbm, eb_hbm, db_hbm, enc_ref, dec_ref,
    pre_f, res_out, gd_out, ag_f, XF,
    xs, ids_ref, cnt_ref, eb_ref, db_ref, F32S, F, X3, XL, WE, WD, PS, PR, SUM, RX, mask_all, mask, act_s, act_f, pre_s,
    T, RB, Q, RQ, RES, RESF, ag_s,
    send, recv, local,
):
    n, X, own, block, width, lanes, flat = dm.n, dm.X, dm.own, dm.block, dm.width, dm.lanes, dm.flat
    rows, lat, chunk = dm.rows, dm.lat, dm.chunk
    depth = n // 2
    L = lax.axis_index("lat")
    t = lax.axis_index("tok")
    c = lax.rem(L, 2)
    chip = L // 2
    y = lax.rem(chip, n)
    z = chip // n
    a = y + c * (z - y)
    b = z + c * (y - z)
    partner = L + 1 - 2 * c

    def lat_of(ap, bp):
        yy = ap + c * (bp - ap)
        zz = bp + c * (ap - bp)
        return (zz * n + yy) * 2 + c

    count = {"copy": 0, "local": 0}
    sends = []

    def wrap(v, m):
        return lax.rem(v + 2 * m, m)

    def remote(src, dst, lat_id, tok_id, recv_index=None):
        k = count["copy"]
        count["copy"] += 1
        r = k if recv_index is None else recv_index
        d = pltpu.make_async_remote_copy(
            src_ref=src, dst_ref=dst, send_sem=send.at[k], recv_sem=recv.at[r],
            device_id=(lat_id, tok_id), device_id_type=MESH,
        )
        return d

    def go(d):
        d.start()
        sends.append(d)
        return d

    def copy_local(src, dst):
        k = count["local"]
        count["local"] += 1
        d = pltpu.make_async_copy(src, dst, local.at[k])
        d.start()
        return d

    x_in = copy_local(x_hbm, xs)

    barrier = pltpu.get_barrier_semaphore()
    heard = 0

    def greet(lat_id, tok_id):
        pl.semaphore_signal(barrier, inc=1, device_id=(lat_id, tok_id), device_id_type=MESH)

    greet(partner, t)
    heard += 1
    for d in range(1, n):
        for other in (0, 1):
            dev = lat_of(wrap(a + d, n), b)
            greet(dev + other * (1 - 2 * c), t)
    heard += 2 * (n - 1)
    for s in (1, -1, 2, -2):
        greet(lat_of(a, wrap(b + s, n)), t)
    heard += 4
    for d in range(1, X):
        for dev in (L, partner):
            greet(dev, wrap(t + d, X))
    heard += 2 * (X - 1)

    x_in.wait()
    xv = xs[...].astype(F32)
    for r in range(own):
        for j in range(2 * lanes):
            at = r * lanes + j % lanes
            F32S[j // lanes, at : at + 1, :] = xv[r : r + 1, j * 128 : (j + 1) * 128]
    for h in (0, 1):
        F[h] = F32S[h].reshape(own, lanes, 128).astype(BF16)

    small_in = [
        copy_local(ids_hbm, ids_ref),
        copy_local(cnt_hbm, cnt_ref),
        copy_local(eb_hbm, eb_ref),
        copy_local(db_hbm, db_ref),
    ]
    pl.semaphore_wait(barrier, heard)

    recv1 = count["copy"]
    count["copy"] += 2 * n

    my_x = X3.at[pl.ds(L * own, own)]
    go(remote(F.at[1 - c], my_x, partner, t, recv1 + c))
    for d in range(1, n):
        for h in (0, 1):
            yy = wrap(y + d, n) if h == 0 else y
            zz = wrap(z + d, n) if h == 1 else z
            go(remote(F.at[h], my_x, (zz * n + yy) * 2 + h, t, recv1 + 2 * d + c))
    my_x[...] = F[c]

    own_cols = pl.ds(pl.multiple_of(c * width, 128), width)
    far_cols = pl.ds(pl.multiple_of((1 - c) * width, 128), width)
    own_lats = pl.ds(pl.multiple_of(c * lat, lat), lat)
    w_local = [copy_local(enc_ref.at[:, own_cols], WE.at[own_lats]), copy_local(dec_ref.at[:, own_cols], WD.at[own_lats])]
    w_remote = [
        go(remote(enc_ref.at[:, far_cols], WE.at[own_lats], partner, t)),
        go(remote(dec_ref.at[:, far_cols], WD.at[own_lats], partner, t)),
    ]

    my_rows = pl.ds(pl.multiple_of(t * chunk, 8), chunk)
    for d in small_in:
        d.wait()
    k_i = lax.broadcasted_iota(jnp.int32, (dm.top, rows), 0)
    local_ids = jnp.where(k_i < jnp.broadcast_to(cnt_ref[...].reshape(1, rows), (dm.top, rows)), ids_ref[...] - L * lat, -1)
    lat_i = lax.broadcasted_iota(jnp.int32, (lat, rows), 0)
    m = jnp.zeros((lat, rows), F32)
    for k in range(dm.top):
        m = jnp.where(local_ids[k : k + 1, :] == lat_i, 1.0, m)
    mask_all[...] = m.T
    mask[...] = mask_all[my_rows, :]

    def block_rows(pos):
        return pl.ds(pl.multiple_of(pos * block, 16), block)

    my_block = block_rows(b)

    def spread(piece, ready):
        by_distance = sorted(range(n), key=lambda d: min(d, n - d))
        first, second = {}, {}

        def push(offset, d, pos):
            ref = piece(wrap(a + d, n), wrap(pos, n))
            return go(remote(ref, ref, lat_of(a, wrap(b + offset, n)), t))

        def level1(d):
            ready(d)
            for offset in (2, -2, 1, -1):
                first[offset, d] = push(offset, d, b)

        def level2(k, d):
            for way in (1, -1):
                first[2 * way, d].wait_recv()
                if (k % 2 == 0) == (way == 1):
                    second[2 * way, d] = push(2 * way, d, b - 2 * way)
                second[way, d] = push(way, d, b - 2 * way)

        for d in by_distance[:5]:
            level1(d)
        level2(0, by_distance[0])
        for d in by_distance[5:]:
            level1(d)
        for k, d in enumerate(by_distance):
            if k:
                level2(k, d)
        for d in by_distance:
            first[1, d].wait_recv()
            first[-1, d].wait_recv()
        for got in second.values():
            got.wait_recv()

    def x_ready(d):
        back = (n - d) % n
        for core in (0, 1) if d else (1 - c,):
            pltpu.make_async_remote_copy(
                src_ref=F.at[0], dst_ref=X3.at[pl.ds(0, own)], send_sem=send.at[0],
                recv_sem=recv.at[recv1 + 2 * back + core], device_id=(partner, t), device_id_type=MESH,
            ).wait_recv()

    def x_piece(ap, bp):
        return X3.at[pl.ds((lat_of(ap, bp) - c) * own, 2 * own)]

    spread(x_piece, x_ready)

    for w in w_local:
        w.wait()
    for w in w_remote:
        w.wait_recv()

    XL[...] = X3[...].astype(F32).reshape(rows * lanes, 128)
    for j in range(lanes):
        XF[c, :, j * 128 : (j + 1) * 128] = XL[pl.ds(j, rows, stride=lanes), :].astype(BF16)
    x_swap = go(remote(XF.at[c], XF.at[c], partner, t))

    order = sorted(range(X), key=lambda d: -min(d, X - d))

    def feature_sum(u, lhs, rhs):
        swap = {}
        arrive = {}
        for d in order:
            part = lax.dot_general(
                lhs(pl.ds(pl.multiple_of(wrap(t + d, X) * chunk, 16), chunk)), rhs, nt, preferred_element_type=F32
            )
            PS[u, d, 0] = part[:, :lat]
            PS[u, d, 1] = part[:, lat:]
            swap[d] = go(remote(PS.at[u, d, 1 - c], PR.at[u, d], partner, t))
        for d in order:
            swap[d].wait_recv()
            SUM[u, d] = PS[u, d, c] + PR[u, d]
            if d:
                arrive[d] = go(remote(SUM.at[u, d], RX.at[u, d - 1], L, wrap(t + d, X)))
        total = SUM[u, 0]
        for d in sorted(arrive, key=lambda d: min(d, X - d)):
            arrive[d].wait_recv()
            total = total + RX[u, d - 1]
        return total

    nt = (((1,), (1,)), ((), ()))
    tn = (((0,), (0,)), ((), ()))
    pre = feature_sum(0, lambda r: XF[c, r, :], WE[...]) + eb_ref[...]
    act_s[...] = (pre * mask[...]).astype(BF16)
    pre_s[...] = pre
    act_rows = pl.ds(pl.multiple_of(t * chunk, 16), chunk)
    act_cols = pl.ds(pl.multiple_of(c * lat, lat), lat)
    act_recv = []
    for d in range(1, X):
        to = wrap(t + d, X)
        for swap in (0, 1):
            dev = L + swap * (1 - 2 * c)
            act_recv.append(go(remote(act_s, act_f.at[act_rows, act_cols], dev, to)))
    act_recv.append(go(remote(act_s, act_f.at[act_rows, act_cols], partner, t)))
    act_f[act_rows, act_cols] = act_s[...]
    pre_recv = []
    for d in range(1, X):
        pre_recv.append(go(remote(pre_s, pre_f.at[my_rows], L, wrap(t + d, X))))
    pre_f[my_rows, :] = pre
    for d in act_recv:
        d.wait_recv()

    def rebuild(pos):
        at = block_rows(pos)
        value = jnp.dot(act_f[at, :], WD[...], preferred_element_type=F32)
        for j in range(lanes):
            T[j, at, :] = value[:, j * 128 : (j + 1) * 128]

    by_way = sorted(range(n), key=lambda d: -min(d, n - d))
    flying = {}

    def hops_of(k, way):
        return depth if (k % 2 == 0) == (way == 1) else depth - 1

    def ring_reduce_hop(i):
        for k, d in enumerate(by_way):
            for way in (1, -1):
                hops = hops_of(k, way)
                if i > hops:
                    continue
                col = wrap(a + d, n)
                at = block_rows(wrap(b + way * (hops + 1 - i), n))
                w = 0 if way == 1 else 1
                if i > 1:
                    flying[way, i - 1, k].wait_recv()
                    T[col, at, :] = T[col, at, :] + RB[w, i - 2, k]
                flying[way, i, k] = go(remote(T.at[col, at], RB.at[w, i - 1, k], lat_of(a, wrap(b + way, n)), t))

    rebuild(wrap(b + depth, n))
    for k in range(depth - 1, 0, -1):
        rebuild(wrap(b + k, n))
        rebuild(wrap(b - k, n))
        if k == depth - 1:
            ring_reduce_hop(1)
    rebuild(b)
    for i in range(2, depth + 1):
        ring_reduce_hop(i)
    q_recv = {}
    for k, d in enumerate(by_way):
        q = T[wrap(a + d, n), my_block, :]
        for way in (1, -1):
            flying[way, hops_of(k, way), k].wait_recv()
            q = q + RB[0 if way == 1 else 1, hops_of(k, way) - 1, k]
        Q[d] = q
        if d:
            q_recv[d] = go(remote(Q.at[d], RQ.at[d - 1], lat_of(wrap(a + d, n), b), t))
    piece = Q[0]
    for d in sorted(q_recv, key=lambda d: min(d, n - d)):
        q_recv[d].wait_recv()
        piece = piece + RQ[d - 1]
    a_cols = pl.ds(pl.multiple_of(a * 128, 128), 128)
    db_cols = pl.ds(pl.multiple_of(c * width + a * 128, 128), 128)
    piece = piece + db_ref[:, db_cols] - XF[c, my_block, a_cols].astype(F32)
    RES[a, my_block, :] = piece.astype(BF16)

    def res_piece(ap, bp):
        return RES.at[ap, block_rows(bp)]

    r_recv = {}
    for d in range(1, n):
        ref = res_piece(a, b)
        r_recv[n - d] = go(remote(ref, ref, lat_of(wrap(a + d, n), b), t))

    def res_ready(d):
        if d:
            r_recv[d].wait_recv()

    spread(res_piece, res_ready)

    r_swap = go(remote(RES, RESF, partner, t))
    back = feature_sum(1, lambda r: jnp.concatenate([RES[j, r, :] for j in range(lanes)], axis=1), WD[...])
    ag_s[...] = (0.5 * back * mask[...]).astype(BF16)
    ag_recv = []
    for d in range(1, X):
        ag_recv.append(go(remote(ag_s, ag_f.at[act_rows], L, wrap(t + d, X))))
    ag_f[act_rows, :] = ag_s[...]

    r_swap.wait_recv()
    x_swap.wait_recv()
    acts = act_f[:, act_cols]
    pick_i = lax.broadcasted_iota(jnp.int32, (16, rows), 0)
    pick_j = lax.broadcasted_iota(jnp.int32, (16, rows), 1)
    pick = jnp.where((pick_i < own) & (pick_j == pick_i + L * own), 1.0, 0.0).astype(BF16)
    for cols, buf in ((own_cols, RES), (far_cols, RESF)):
        value = jnp.concatenate([buf[j] for j in range(lanes)], axis=1)
        gd_out[:, cols] = (0.5 * lax.dot_general(acts, value, tn, preferred_element_type=F32)).astype(BF16)
        res_out[:, cols] = jnp.dot(pick, value, preferred_element_type=F32)[:own].astype(BF16)
    for d in pre_recv:
        d.wait_recv()
    for d in ag_recv:
        d.wait_recv()
    for d in sends:
        d.wait_send()


def finish(pre_ref, res_ref, gd_ref, ag_ref, xf_ref, pre_out, res_out, ge_out, gd_out, ge_s, sems):
    moves = [
        pltpu.make_async_copy(pre_ref, pre_out, sems.at[0]),
        pltpu.make_async_copy(res_ref, res_out, sems.at[1]),
        pltpu.make_async_copy(gd_ref, gd_out, sems.at[2]),
    ]
    for d in moves:
        d.start()
    width = ge_s.shape[2]
    grads = ag_ref[...]
    for h in (0, 1):
        ge_s[h] = lax.dot_general(
            grads, xf_ref[h], (((0,), (0,)), ((), ())), preferred_element_type=F32
        ).astype(BF16)
        d = pltpu.make_async_copy(ge_s.at[h], ge_out.at[:, pl.ds(h * width, width)], sems.at[3 + h])
        d.start()
        moves.append(d)
    for d in moves:
        d.wait()


def shards(mesh, resid_stream, enc_weight, enc_bias, dec_weight, dec_bias, active_ids, active_count):
    own, width = resid_stream.shape
    lat = enc_weight.shape[0]
    dm = Dims(mesh, own, width, lat, active_ids.shape[1])
    n, rows, block, w = dm.n, dm.rows, dm.block, dm.width
    vmem = pl.BlockSpec(memory_space=pltpu.VMEM)
    hbm = pl.BlockSpec(memory_space=pltpu.HBM)
    copies = 288
    pre, res, gd, ag, xf = pl.pallas_call(
        functools.partial(kernel, dm),
        out_shape=(
            jax.ShapeDtypeStruct((rows, lat), F32),
            jax.ShapeDtypeStruct((own, width), BF16),
            jax.ShapeDtypeStruct((lat, width), BF16),
            jax.ShapeDtypeStruct((rows, lat), BF16),
            jax.ShapeDtypeStruct((2, rows, w), BF16),
        ),
        in_specs=[hbm] * 7,
        out_specs=(vmem,) * 5,
        scratch_shapes=[
            pltpu.VMEM((own, width), BF16),
            pltpu.VMEM((dm.top, rows), jnp.int32),
            pltpu.VMEM((rows,), jnp.int32),
            pltpu.VMEM((1, lat), F32),
            pltpu.VMEM((1, width), F32),
            pltpu.VMEM((2, dm.flat, 128), F32),
            pltpu.VMEM((2, own, dm.lanes, 128), BF16),
            pltpu.VMEM((rows, dm.lanes, 128), BF16),
            pltpu.VMEM((rows * dm.lanes, 128), F32),
            pltpu.VMEM((2 * lat, w), BF16),
            pltpu.VMEM((2 * lat, w), BF16),
            pltpu.VMEM((2, dm.X, 2, dm.chunk, lat), F32),
            pltpu.VMEM((2, dm.X, dm.chunk, lat), F32),
            pltpu.VMEM((2, dm.X, dm.chunk, lat), F32),
            pltpu.VMEM((2, dm.X - 1, dm.chunk, lat), F32),
            pltpu.VMEM((rows, lat), F32),
            pltpu.VMEM((dm.chunk, lat), F32),
            pltpu.VMEM((dm.chunk, lat), BF16),
            pltpu.VMEM((rows, 2 * lat), BF16),
            pltpu.VMEM((dm.chunk, lat), F32),
            pltpu.VMEM((dm.lanes, rows, 128), F32),
            pltpu.VMEM((2, n // 2, n, block, 128), F32),
            pltpu.VMEM((n, block, 128), F32),
            pltpu.VMEM((n - 1, block, 128), F32),
            pltpu.VMEM((dm.lanes, rows, 128), BF16),
            pltpu.VMEM((dm.lanes, rows, 128), BF16),
            pltpu.VMEM((dm.chunk, lat), BF16),
            pltpu.SemaphoreType.DMA((copies,)),
            pltpu.SemaphoreType.DMA((copies,)),
            pltpu.SemaphoreType.DMA((8,)),
        ],
        compiler_params=pltpu.CompilerParams(
            collective_id=0, has_side_effects=True, vmem_limit_bytes=48 * 1024 * 1024
        ),
    )(
        *(
            pltpu.with_memory_space_constraint(v, pltpu.HBM)
            for v in (
                resid_stream,
                active_ids.T,
                active_count,
                enc_bias.reshape(1, lat),
                dec_bias.reshape(1, width),
                enc_weight,
                dec_weight,
            )
        )
    )
    return pl.pallas_call(
        finish,
        out_shape=(
            jax.ShapeDtypeStruct((rows, lat), F32),
            jax.ShapeDtypeStruct((own, width), BF16),
            jax.ShapeDtypeStruct((lat, width), BF16),
            jax.ShapeDtypeStruct((lat, width), BF16),
        ),
        in_specs=[vmem] * 5,
        out_specs=(hbm,) * 4,
        scratch_shapes=[pltpu.VMEM((2, lat, w), BF16), pltpu.SemaphoreType.DMA((5,))],
        compiler_params=pltpu.CompilerParams(vmem_limit_bytes=4 * 1024 * 1024),
    )(pre, res, gd, ag, xf)


def solution(mesh):
    placed = (P("lat", "tok"), P("lat", "tok"), P("lat"), P("lat", "tok"), P("tok"), P(), P())
    return jax.shard_map(
        functools.partial(shards, mesh),
        mesh=mesh,
        in_specs=placed,
        out_specs=(P(None, "lat"), P("lat", "tok"), P("lat", "tok"), P("lat", "tok")),
        check_vma=False,
    )
```

```python
import functools
import math

import jax
import jax.numpy as jnp
from jax import lax
from jax.experimental import pallas as pl
from jax.experimental.pallas import tpu as pltpu
from jax.sharding import PartitionSpec as P

F32 = jnp.float32
BF16 = jnp.bfloat16
MESH = pl.DeviceIdType.MESH


class Dims:
    def __init__(self, mesh, rows_own, width, lat_dev, top_count):
        self.X = mesh.shape["tok"]
        self.n = math.isqrt(mesh.shape["lat"] // 2)
        assert self.n == 8 and self.n * self.n * 2 == mesh.shape["lat"]
        self.own = rows_own
        self.rows = rows_own * mesh.shape["lat"]
        self.block = self.rows // self.n
        self.width = width // 2
        self.lanes = self.width // 128
        self.flat = rows_own * self.lanes
        self.lat = lat_dev
        self.top = top_count
        self.chunk = self.rows // self.X


def kernel(
    dm,
    x_hbm, ids_hbm, cnt_hbm, eb_hbm, db_hbm, enc_ref, dec_ref,
    pre_f, res_out, gd_out, ag_f, XF,
    xs, ids_ref, cnt_ref, eb_ref, db_ref, F32S, F, X3, XL, WE, WD, PS, PR, SUM, RX, mask_all, mask, act_s, act_f, pre_s,
    T, RB, RF, Q, RQ, RES, RESF, ag_s,
    send, recv, local,
):
    n, X, own, block, width, lanes, flat = dm.n, dm.X, dm.own, dm.block, dm.width, dm.lanes, dm.flat
    rows, lat, chunk = dm.rows, dm.lat, dm.chunk
    depth = n // 2
    L = lax.axis_index("lat")
    t = lax.axis_index("tok")
    c = lax.rem(L, 2)
    chip = L // 2
    y = lax.rem(chip, n)
    z = chip // n
    a = y + c * (z - y)
    b = z + c * (y - z)
    partner = L + 1 - 2 * c

    def lat_of(ap, bp):
        yy = ap + c * (bp - ap)
        zz = bp + c * (ap - bp)
        return (zz * n + yy) * 2 + c

    count = {"copy": 0, "local": 0}
    sends = []

    def wrap(v, m):
        return lax.rem(v + 2 * m, m)

    def remote(src, dst, lat_id, tok_id, recv_index=None):
        k = count["copy"]
        count["copy"] += 1
        r = k if recv_index is None else recv_index
        d = pltpu.make_async_remote_copy(
            src_ref=src, dst_ref=dst, send_sem=send.at[k], recv_sem=recv.at[r],
            device_id=(lat_id, tok_id), device_id_type=MESH,
        )
        return d

    def go(d):
        d.start()
        sends.append(d)
        return d

    def copy_local(src, dst):
        k = count["local"]
        count["local"] += 1
        d = pltpu.make_async_copy(src, dst, local.at[k])
        d.start()
        return d

    x_in = copy_local(x_hbm, xs)

    barrier = pltpu.get_barrier_semaphore()
    heard = 0

    def greet(lat_id, tok_id):
        pl.semaphore_signal(barrier, inc=1, device_id=(lat_id, tok_id), device_id_type=MESH)

    greet(partner, t)
    heard += 1
    for d in range(1, n):
        for other in (0, 1):
            dev = lat_of(wrap(a + d, n), b)
            greet(dev + other * (1 - 2 * c), t)
    heard += 2 * (n - 1)
    for s in (1, -1, 2, -2):
        greet(lat_of(a, wrap(b + s, n)), t)
    heard += 4
    for d in range(1, X):
        for dev in (L, partner):
            greet(dev, wrap(t + d, X))
    heard += 2 * (X - 1)

    x_in.wait()
    xv = xs[...].astype(F32)
    for r in range(own):
        for j in range(2 * lanes):
            at = r * lanes + j % lanes
            F32S[j // lanes, at : at + 1, :] = xv[r : r + 1, j * 128 : (j + 1) * 128]
    for h in (0, 1):
        F[h] = F32S[h].reshape(own, lanes, 128).astype(BF16)

    small_in = [
        copy_local(ids_hbm, ids_ref),
        copy_local(cnt_hbm, cnt_ref),
        copy_local(eb_hbm, eb_ref),
        copy_local(db_hbm, db_ref),
    ]
    pl.semaphore_wait(barrier, heard)

    recv1 = count["copy"]
    count["copy"] += 2 * n

    my_x = X3.at[pl.ds(L * own, own)]
    go(remote(F.at[1 - c], my_x, partner, t, recv1 + c))
    for d in range(1, n):
        for h in (0, 1):
            yy = wrap(y + d, n) if h == 0 else y
            zz = wrap(z + d, n) if h == 1 else z
            go(remote(F.at[h], my_x, (zz * n + yy) * 2 + h, t, recv1 + 2 * d + c))
    my_x[...] = F[c]

    own_cols = pl.ds(pl.multiple_of(c * width, 128), width)
    far_cols = pl.ds(pl.multiple_of((1 - c) * width, 128), width)
    own_lats = pl.ds(pl.multiple_of(c * lat, lat), lat)
    w_local = [copy_local(enc_ref.at[:, own_cols], WE.at[own_lats]), copy_local(dec_ref.at[:, own_cols], WD.at[own_lats])]
    w_remote = [
        go(remote(enc_ref.at[:, far_cols], WE.at[own_lats], partner, t)),
        go(remote(dec_ref.at[:, far_cols], WD.at[own_lats], partner, t)),
    ]

    my_rows = pl.ds(pl.multiple_of(t * chunk, 8), chunk)
    for d in small_in:
        d.wait()
    k_i = lax.broadcasted_iota(jnp.int32, (dm.top, rows), 0)
    local_ids = jnp.where(k_i < jnp.broadcast_to(cnt_ref[...].reshape(1, rows), (dm.top, rows)), ids_ref[...] - L * lat, -1)
    lat_i = lax.broadcasted_iota(jnp.int32, (lat, rows), 0)
    m = jnp.zeros((lat, rows), F32)
    for k in range(dm.top):
        m = jnp.where(local_ids[k : k + 1, :] == lat_i, 1.0, m)
    mask_all[...] = m.T
    mask[...] = mask_all[my_rows, :]

    def block_rows(pos):
        return pl.ds(pl.multiple_of(pos * block, 16), block)

    my_block = block_rows(b)

    def spread(piece, ready):
        by_distance = sorted(range(n), key=lambda d: min(d, n - d))
        first, second = {}, {}

        def push(offset, d, pos):
            ref = piece(wrap(a + d, n), wrap(pos, n))
            return go(remote(ref, ref, lat_of(a, wrap(b + offset, n)), t))

        def level1(d):
            ready(d)
            for offset in (2, -2, 1, -1):
                first[offset, d] = push(offset, d, b)

        def level2(k, d):
            for way in (1, -1):
                first[2 * way, d].wait_recv()
                if (k % 2 == 0) == (way == 1):
                    second[2 * way, d] = push(2 * way, d, b - 2 * way)
                second[way, d] = push(way, d, b - 2 * way)

        for d in by_distance[:5]:
            level1(d)
        level2(0, by_distance[0])
        for d in by_distance[5:]:
            level1(d)
        for k, d in enumerate(by_distance):
            if k:
                level2(k, d)
        for d in by_distance:
            first[1, d].wait_recv()
            first[-1, d].wait_recv()
        for got in second.values():
            got.wait_recv()

    def x_ready(d):
        back = (n - d) % n
        for core in (0, 1) if d else (1 - c,):
            pltpu.make_async_remote_copy(
                src_ref=F.at[0], dst_ref=X3.at[pl.ds(0, own)], send_sem=send.at[0],
                recv_sem=recv.at[recv1 + 2 * back + core], device_id=(partner, t), device_id_type=MESH,
            ).wait_recv()

    def x_piece(ap, bp):
        return X3.at[pl.ds((lat_of(ap, bp) - c) * own, 2 * own)]

    spread(x_piece, x_ready)

    for w in w_local:
        w.wait()
    for w in w_remote:
        w.wait_recv()

    XL[...] = X3[...].astype(F32).reshape(rows * lanes, 128)
    for j in range(lanes):
        XF[c, :, j * 128 : (j + 1) * 128] = XL[pl.ds(j, rows, stride=lanes), :].astype(BF16)
    x_swap = go(remote(XF.at[c], XF.at[c], partner, t))

    order = sorted(range(X), key=lambda d: -min(d, X - d))

    def feature_sum(u, lhs, rhs):
        swap = {}
        arrive = {}
        for d in order:
            part = lax.dot_general(
                lhs(pl.ds(pl.multiple_of(wrap(t + d, X) * chunk, 16), chunk)), rhs, nt, preferred_element_type=F32
            )
            PS[u, d, 0] = part[:, :lat]
            PS[u, d, 1] = part[:, lat:]
            swap[d] = go(remote(PS.at[u, d, 1 - c], PR.at[u, d], partner, t))
        for d in order:
            swap[d].wait_recv()
            SUM[u, d] = PS[u, d, c] + PR[u, d]
            if d:
                arrive[d] = go(remote(SUM.at[u, d], RX.at[u, d - 1], L, wrap(t + d, X)))
        total = SUM[u, 0]
        for d in sorted(arrive, key=lambda d: min(d, X - d)):
            arrive[d].wait_recv()
            total = total + RX[u, d - 1]
        return total

    nt = (((1,), (1,)), ((), ()))
    tn = (((0,), (0,)), ((), ()))
    pre = feature_sum(0, lambda r: XF[c, r, :], WE[...]) + eb_ref[...]
    act_s[...] = (pre * mask[...]).astype(BF16)
    pre_s[...] = pre
    act_rows = pl.ds(pl.multiple_of(t * chunk, 16), chunk)
    act_cols = pl.ds(pl.multiple_of(c * lat, lat), lat)
    act_recv = []
    for d in range(1, X):
        to = wrap(t + d, X)
        for swap in (0, 1):
            dev = L + swap * (1 - 2 * c)
            act_recv.append(go(remote(act_s, act_f.at[act_rows, act_cols], dev, to)))
    act_recv.append(go(remote(act_s, act_f.at[act_rows, act_cols], partner, t)))
    act_f[act_rows, act_cols] = act_s[...]
    pre_recv = []
    for d in range(1, X):
        pre_recv.append(go(remote(pre_s, pre_f.at[my_rows], L, wrap(t + d, X))))
    pre_f[my_rows, :] = pre
    for d in act_recv:
        d.wait_recv()

    def rebuild(pos):
        at = block_rows(pos)
        value = jnp.dot(act_f[at, :], WD[...], preferred_element_type=F32)
        for j in range(lanes):
            T[j, at, :] = value[:, j * 128 : (j + 1) * 128]

    by_way = sorted(range(n), key=lambda d: -min(d, n - d))
    flying = {}

    def send_far():
        col_rows = block_rows(wrap(b + depth, n))
        for k, d in enumerate(by_way):
            way = 1 if k % 2 == 0 else -1
            flying[way, 0, k] = go(
                remote(T.at[wrap(a + d, n), col_rows], RF.at[k], lat_of(a, wrap(b + 2 * way, n)), t)
            )

    def ring_reduce_hop(i):
        for k, d in enumerate(by_way):
            col = wrap(a + d, n)
            for way in (1, -1):
                at = block_rows(wrap(b + way * (depth - i), n))
                w = 0 if way == 1 else 1
                if i > 1:
                    flying[way, i - 1, k].wait_recv()
                    value = T[col, at, :] + RB[w, i - 2, k]
                    if i == 2 and (way, 0, k) in flying:
                        flying[way, 0, k].wait_recv()
                        value = value + RF[k]
                    T[col, at, :] = value
                flying[way, i, k] = go(remote(T.at[col, at], RB.at[w, i - 1, k], lat_of(a, wrap(b + way, n)), t))

    rebuild(wrap(b + depth, n))
    send_far()
    for k in range(depth - 1, 0, -1):
        rebuild(wrap(b + k, n))
        rebuild(wrap(b - k, n))
        if k == depth - 1:
            ring_reduce_hop(1)
    rebuild(b)
    for i in range(2, depth):
        ring_reduce_hop(i)
    q_recv = {}
    for k, d in enumerate(by_way):
        q = T[wrap(a + d, n), my_block, :]
        for way in (1, -1):
            flying[way, depth - 1, k].wait_recv()
            q = q + RB[0 if way == 1 else 1, depth - 2, k]
        Q[d] = q
        if d:
            q_recv[d] = go(remote(Q.at[d], RQ.at[d - 1], lat_of(wrap(a + d, n), b), t))
    piece = Q[0]
    for d in sorted(q_recv, key=lambda d: min(d, n - d)):
        q_recv[d].wait_recv()
        piece = piece + RQ[d - 1]
    a_cols = pl.ds(pl.multiple_of(a * 128, 128), 128)
    db_cols = pl.ds(pl.multiple_of(c * width + a * 128, 128), 128)
    piece = piece + db_ref[:, db_cols] - XF[c, my_block, a_cols].astype(F32)
    RES[a, my_block, :] = piece.astype(BF16)

    def res_piece(ap, bp):
        return RES.at[ap, block_rows(bp)]

    r_recv = {}
    for d in range(1, n):
        ref = res_piece(a, b)
        r_recv[n - d] = go(remote(ref, ref, lat_of(wrap(a + d, n), b), t))

    def res_ready(d):
        if d:
            r_recv[d].wait_recv()

    spread(res_piece, res_ready)

    r_swap = go(remote(RES, RESF, partner, t))
    back = feature_sum(1, lambda r: jnp.concatenate([RES[j, r, :] for j in range(lanes)], axis=1), WD[...])
    ag_s[...] = (0.5 * back * mask[...]).astype(BF16)
    ag_recv = []
    for d in range(1, X):
        ag_recv.append(go(remote(ag_s, ag_f.at[act_rows], L, wrap(t + d, X))))
    ag_f[act_rows, :] = ag_s[...]

    r_swap.wait_recv()
    x_swap.wait_recv()
    acts = act_f[:, act_cols]
    pick_i = lax.broadcasted_iota(jnp.int32, (16, rows), 0)
    pick_j = lax.broadcasted_iota(jnp.int32, (16, rows), 1)
    pick = jnp.where((pick_i < own) & (pick_j == pick_i + L * own), 1.0, 0.0).astype(BF16)
    for cols, buf in ((own_cols, RES), (far_cols, RESF)):
        value = jnp.concatenate([buf[j] for j in range(lanes)], axis=1)
        gd_out[:, cols] = (0.5 * lax.dot_general(acts, value, tn, preferred_element_type=F32)).astype(BF16)
        res_out[:, cols] = jnp.dot(pick, value, preferred_element_type=F32)[:own].astype(BF16)
    for d in pre_recv:
        d.wait_recv()
    for d in ag_recv:
        d.wait_recv()
    for d in sends:
        d.wait_send()


def finish(pre_ref, res_ref, gd_ref, ag_ref, xf_ref, pre_out, res_out, ge_out, gd_out, ge_s, sems):
    moves = [
        pltpu.make_async_copy(pre_ref, pre_out, sems.at[0]),
        pltpu.make_async_copy(res_ref, res_out, sems.at[1]),
        pltpu.make_async_copy(gd_ref, gd_out, sems.at[2]),
    ]
    for d in moves:
        d.start()
    width = ge_s.shape[2]
    grads = ag_ref[...]
    for h in (0, 1):
        ge_s[h] = lax.dot_general(
            grads, xf_ref[h], (((0,), (0,)), ((), ())), preferred_element_type=F32
        ).astype(BF16)
        d = pltpu.make_async_copy(ge_s.at[h], ge_out.at[:, pl.ds(h * width, width)], sems.at[3 + h])
        d.start()
        moves.append(d)
    for d in moves:
        d.wait()


def shards(mesh, resid_stream, enc_weight, enc_bias, dec_weight, dec_bias, active_ids, active_count):
    own, width = resid_stream.shape
    lat = enc_weight.shape[0]
    dm = Dims(mesh, own, width, lat, active_ids.shape[1])
    n, rows, block, w = dm.n, dm.rows, dm.block, dm.width
    vmem = pl.BlockSpec(memory_space=pltpu.VMEM)
    hbm = pl.BlockSpec(memory_space=pltpu.HBM)
    copies = 288
    pre, res, gd, ag, xf = pl.pallas_call(
        functools.partial(kernel, dm),
        out_shape=(
            jax.ShapeDtypeStruct((rows, lat), F32),
            jax.ShapeDtypeStruct((own, width), BF16),
            jax.ShapeDtypeStruct((lat, width), BF16),
            jax.ShapeDtypeStruct((rows, lat), BF16),
            jax.ShapeDtypeStruct((2, rows, w), BF16),
        ),
        in_specs=[hbm] * 7,
        out_specs=(vmem,) * 5,
        scratch_shapes=[
            pltpu.VMEM((own, width), BF16),
            pltpu.VMEM((dm.top, rows), jnp.int32),
            pltpu.VMEM((rows,), jnp.int32),
            pltpu.VMEM((1, lat), F32),
            pltpu.VMEM((1, width), F32),
            pltpu.VMEM((2, dm.flat, 128), F32),
            pltpu.VMEM((2, own, dm.lanes, 128), BF16),
            pltpu.VMEM((rows, dm.lanes, 128), BF16),
            pltpu.VMEM((rows * dm.lanes, 128), F32),
            pltpu.VMEM((2 * lat, w), BF16),
            pltpu.VMEM((2 * lat, w), BF16),
            pltpu.VMEM((2, dm.X, 2, dm.chunk, lat), F32),
            pltpu.VMEM((2, dm.X, dm.chunk, lat), F32),
            pltpu.VMEM((2, dm.X, dm.chunk, lat), F32),
            pltpu.VMEM((2, dm.X - 1, dm.chunk, lat), F32),
            pltpu.VMEM((rows, lat), F32),
            pltpu.VMEM((dm.chunk, lat), F32),
            pltpu.VMEM((dm.chunk, lat), BF16),
            pltpu.VMEM((rows, 2 * lat), BF16),
            pltpu.VMEM((dm.chunk, lat), F32),
            pltpu.VMEM((dm.lanes, rows, 128), F32),
            pltpu.VMEM((2, n // 2 - 1, n, block, 128), F32),
            pltpu.VMEM((n, block, 128), F32),
            pltpu.VMEM((n, block, 128), F32),
            pltpu.VMEM((n - 1, block, 128), F32),
            pltpu.VMEM((dm.lanes, rows, 128), BF16),
            pltpu.VMEM((dm.lanes, rows, 128), BF16),
            pltpu.VMEM((dm.chunk, lat), BF16),
            pltpu.SemaphoreType.DMA((copies,)),
            pltpu.SemaphoreType.DMA((copies,)),
            pltpu.SemaphoreType.DMA((8,)),
        ],
        compiler_params=pltpu.CompilerParams(
            collective_id=0, has_side_effects=True, vmem_limit_bytes=48 * 1024 * 1024
        ),
    )(
        *(
            pltpu.with_memory_space_constraint(v, pltpu.HBM)
            for v in (
                resid_stream,
                active_ids.T,
                active_count,
                enc_bias.reshape(1, lat),
                dec_bias.reshape(1, width),
                enc_weight,
                dec_weight,
            )
        )
    )
    return pl.pallas_call(
        finish,
        out_shape=(
            jax.ShapeDtypeStruct((rows, lat), F32),
            jax.ShapeDtypeStruct((own, width), BF16),
            jax.ShapeDtypeStruct((lat, width), BF16),
            jax.ShapeDtypeStruct((lat, width), BF16),
        ),
        in_specs=[vmem] * 5,
        out_specs=(hbm,) * 4,
        scratch_shapes=[pltpu.VMEM((2, lat, w), BF16), pltpu.SemaphoreType.DMA((5,))],
        compiler_params=pltpu.CompilerParams(vmem_limit_bytes=4 * 1024 * 1024),
    )(pre, res, gd, ag, xf)


def solution(mesh):
    placed = (P("lat", "tok"), P("lat", "tok"), P("lat"), P("lat", "tok"), P("tok"), P(), P())
    return jax.shard_map(
        functools.partial(shards, mesh),
        mesh=mesh,
        in_specs=placed,
        out_specs=(P(None, "lat"), P("lat", "tok"), P("lat", "tok"), P("lat", "tok")),
        check_vma=False,
    )
```
